128 devices in a mesh: seq: 16 (over z, x_hi, core), head: 8 (over y, x_lo).
Axes of the slice: x: 4 (x_hi: 2, x_lo: 2; x = x_hi * 2 + x_lo), y: 4, z: 4, core: 2. Of those that a mesh axis runs over, the one named last changes fastest.
Arguments:
- x_values: bfloat16 [16384, 16384], P('seq', 'head'), may hold values from -6 to 6
- bc_values: bfloat16 [2, 16384, 2048], P(None, 'seq', 'head'), may hold values from -6 to 6
- z_values: bfloat16 [16384, 16384], P('seq', 'head'), may hold values from -12 to 12
- dt_values: bfloat16 [16384, 256], P('seq', 'head'), may hold values from -4 to 4
- xconv_weight: float32 [4, 16384], P(None, 'head'), may hold values from -3 to 3
- bconv_weight: float32 [2, 4, 2048], P(None, None, 'head'), may hold values from -3 to 3
- xconv_bias: float32 [16384], P('head'), may hold values from -0.5 to 0.5
- bconv_bias: float32 [2, 2048], P(None, 'head'), may hold values from -0.5 to 0.5
- dt_offset: float32 [256], P('head'), may hold values from -16 to -3
- decay_log: float32 [256], P('head'), may hold values from 0 to 3
- skip_gain: float32 [256], P('head'), may hold values from 0.5 to 2
- norm_gain: float32 [16384], P('head'), may hold values from 0.1 to 1.9
- out_weight: bfloat16 [16384, 4096], P('head'), may hold values from -0.046875 to 0.046875
Outputs:
- mixer_out: bfloat16 [16384, 4096], P(('seq', 'head'))
The draws below stay inside these ranges and needn't reach their ends.
All inputs are finite; a program needn't handle non-finite values.
Results may differ from the reference program's by a relative error of at most 0.015.
Values may be sent and summed in bfloat16 or wider, within the bound.
A program may use at most 256 MiB of HBM per device.

```python
import math
import jax
import jax.numpy as jnp
from jax import lax

H = 256
P_SIZE = 64
N = 256
G = 8
KW = 4
BLOCK = 128
DOUT = 4096
TOKENS = 16384


def decay_params(key):
    base = jax.random.fold_in(key, 11)
    key_kind, key_size, key_rate = jax.random.split(base, 3)
    slow = jax.random.randint(key_kind, (H,), 0, 2) > 0
    magnitude = jnp.exp(jax.random.uniform(key_size, (H,), jnp.float32, 0.0, jnp.log(16.0)))
    pick = jax.random.uniform(key_rate, (H,), jnp.float32)
    slow_rate = jnp.exp(jnp.log(0.4) + pick * (jnp.log(1.4) - jnp.log(0.4))) / TOKENS
    fast_rate = 1.0 / (30.0 * jnp.exp(pick * jnp.log(50.0 / 30.0)))
    rate = jnp.where(slow, slow_rate, fast_rate)
    offset = jnp.log(rate / (magnitude * 1.65))
    return (jnp.log(magnitude).astype(jnp.float32), offset.astype(jnp.float32))


def draw_decay_log(key, part):
    return decay_params(key)[0]


def draw_dt_offset(key, part):
    return decay_params(key)[1]


def shared_latent(key):
    base = jax.random.fold_in(key, 21)
    key_value = jax.random.fold_in(base, 0)
    runs = TOKENS // 4
    latent = jax.random.normal(key_value, (runs, P_SIZE), jnp.float32)
    return jnp.repeat(latent, 4, axis=0)


def own_noise(key, shape):
    return 0.3 * jax.random.normal(key, shape, jnp.float32)


def signed_amplitude(key, count):
    key_sign, key_size = jax.random.split(key, 2)
    sign = (jax.random.randint(key_sign, (count,), 0, 2) * 2 - 1).astype(jnp.float32)
    return sign * jax.random.uniform(key_size, (count,), jnp.float32, 0.7, 1.3)


def draw_x_values(key, part):
    latent = shared_latent(key)
    base = jax.random.fold_in(key, 22)
    key_perm, key_amp, key_noise = jax.random.split(base, 3)
    orders = jax.vmap(lambda sub: jax.random.permutation(sub, P_SIZE))(jax.random.split(key_perm, H))
    index = orders.reshape(H * P_SIZE).astype(jnp.int32)
    amplitude = signed_amplitude(key_amp, H * P_SIZE)
    values = jnp.take(latent, index, axis=1) * amplitude[None, :] + own_noise(key_noise, (TOKENS, H * P_SIZE))
    return jnp.clip(values, -6.0, 6.0).astype(jnp.bfloat16)


def draw_bc_values(key, part):
    latent = shared_latent(key)
    base = jax.random.fold_in(key, 23)
    key_perm, key_amp, key_noise, key_other = jax.random.split(base, 4)
    orders = jax.vmap(lambda sub: jax.random.permutation(sub, N))(jax.random.split(key_perm, G))
    index = (orders.reshape(G * N) % P_SIZE).astype(jnp.int32)
    amplitude = signed_amplitude(key_amp, G * N)
    b_part = jnp.take(latent, index, axis=1) * amplitude[None, :] + own_noise(key_noise, (TOKENS, G * N))
    c_part = jax.random.normal(key_other, (TOKENS, G * N), jnp.float32)
    values = jnp.stack([b_part, c_part], axis=0)
    return jnp.clip(values, -6.0, 6.0).astype(jnp.bfloat16)


def draw_z_values(key, part):
    base = jax.random.fold_in(key, 5)
    key_col = jax.random.fold_in(base, 0)
    key_val = jax.random.fold_in(base, 2)
    column = 0.3 * jnp.exp(jax.random.uniform(key_col, (H * P_SIZE,), jnp.float32, 0.0, jnp.log(10.0)))
    values = jax.random.normal(key_val, (TOKENS, H * P_SIZE), jnp.float32) * column[None, :]
    return jnp.clip(values, -12.0, 12.0).astype(jnp.bfloat16)


def block_levels(own_key, dims, pieces, smallest, high):
    def one(axis_at, blocks):
        draws = jax.random.uniform(jax.random.fold_in(jax.random.fold_in(own_key, 6), axis_at), (blocks,), jnp.float32, smallest / len(pieces), high / len(pieces))
        return jnp.repeat(jnp.exp(draws), dims[axis_at] // blocks).reshape((-1,) + (1,) * (len(dims) - axis_at - 1))

    gain = one(*pieces[0])
    for cut in pieces[1:]:
        gain = gain * one(*cut)
    return gain


def normal_values(key, extent, deviation, reach, cuts=(), held_as=jnp.bfloat16):
    values = jax.random.normal(key, extent, jnp.float32) * deviation
    if len(cuts) > 0:
        values = block_levels(key, extent, cuts, -0.22, 0.18) * values
    return jnp.clip(values, min=-reach, max=reach).astype(held_as)


def setup_inputs(seed: int = 0) -> dict:
    seeds = jax.random.split(jax.random.key(seed), 14)
    return {
        "x_values": draw_x_values(jax.random.fold_in(seeds[13], 71), 0),
        "bc_values": draw_bc_values(jax.random.fold_in(seeds[13], 71), 0),
        "z_values": draw_z_values(jax.random.fold_in(seeds[13], 71), 0),
        "dt_values": normal_values(seeds[3], (TOKENS, H), 1.0, 4.0, ((0, 16), (1, 8))),
        "xconv_weight": normal_values(seeds[4], (KW, H * P_SIZE), KW ** -0.5, 3.0, ((1, 8),), jnp.float32),
        "bconv_weight": normal_values(seeds[5], (2, KW, G * N), KW ** -0.5, 3.0, ((2, 8),), jnp.float32),
        "xconv_bias": jnp.clip(jax.random.uniform(seeds[6], (H * P_SIZE,), jnp.float32, -0.5, 0.5) * block_levels(seeds[6], (H * P_SIZE,), ((0, 8),), -0.4, 0.0), -0.5, 0.5),
        "bconv_bias": jnp.clip(jax.random.uniform(seeds[7], (2, G * N), jnp.float32, -0.5, 0.5) * block_levels(seeds[7], (2, G * N), ((1, 8),), -0.4, 0.0), -0.5, 0.5),
        "dt_offset": draw_dt_offset(jax.random.fold_in(seeds[13], 71), 0),
        "decay_log": draw_decay_log(jax.random.fold_in(seeds[13], 71), 0),
        "skip_gain": jnp.clip(jnp.exp(math.log(2.0) - 1.3862944 * jax.random.uniform(seeds[10], (H,), jnp.float32) ** block_levels(seeds[10], (H,), ((0, 8),), -0.2, 0.2)), 0.5, 2.0),
        "norm_gain": jnp.clip(1.0 + 0.18 * jax.random.normal(seeds[11], (H * P_SIZE,), jnp.float32), 0.1, 1.9),
        "out_weight": normal_values(seeds[12], (H * P_SIZE, DOUT), (H * P_SIZE) ** -0.5, 0.046875, ((0, 8),)),
    }


def conv_silu(values, weight, bias):
    length = values.shape[0]
    padded = jnp.pad(values.astype(jnp.float32), ((KW - 1, 0), (0, 0)))
    total = jnp.zeros((length, values.shape[1]), jnp.float32) + bias[None, :]
    for offset in range(KW):
        total = total + weight[offset][None, :] * padded[offset:offset + length]
    return jax.nn.silu(total).astype(jnp.bfloat16)

def reference(x_values, bc_values, z_values, dt_values, xconv_weight, bconv_weight, xconv_bias, bconv_bias, dt_offset, decay_log, skip_gain, norm_gain, out_weight):
    x_conv = conv_silu(x_values, xconv_weight, xconv_bias)
    b_conv = conv_silu(bc_values[0], bconv_weight[0], bconv_bias[0])
    c_conv = conv_silu(bc_values[1], bconv_weight[1], bconv_bias[1])
    steps_dt = jax.nn.softplus(dt_values.astype(jnp.float32) + dt_offset[None, :])
    log_decay = steps_dt * (-jnp.exp(decay_log))[None, :]
    per_group = H // G
    blocks = TOKENS // BLOCK
    width = per_group * P_SIZE
    positions = jnp.arange(BLOCK)
    causal = (positions[:, None] >= positions[None, :])[None, :, :, None]

    def one_group(group):
        group = group.astype(jnp.int32)
        x_part = lax.dynamic_slice_in_dim(x_conv, group * width, width, 1).reshape(blocks, BLOCK, per_group, P_SIZE)
        b_part = lax.dynamic_slice_in_dim(b_conv, group * N, N, 1).reshape(blocks, BLOCK, N)
        c_part = lax.dynamic_slice_in_dim(c_conv, group * N, N, 1).reshape(blocks, BLOCK, N)
        dt_part = lax.dynamic_slice_in_dim(steps_dt, group * per_group, per_group, 1).reshape(blocks, BLOCK, per_group)
        decay_part = lax.dynamic_slice_in_dim(log_decay, group * per_group, per_group, 1).reshape(blocks, BLOCK, per_group)
        cumul = jnp.cumsum(decay_part, axis=1)
        inner = jnp.einsum('ctn,csn->cts', c_part.astype(jnp.float32), b_part.astype(jnp.float32))
        diff = cumul[:, :, None, :] - cumul[:, None, :, :]
        weights = jnp.where(causal, jnp.exp(jnp.where(causal, diff, 0.0)), 0.0)
        scores = (inner[..., None] * weights * dt_part[:, None, :, :]).astype(jnp.bfloat16)
        y_intra = jnp.einsum('ctsh,cshp->cthp', scores.astype(jnp.float32), x_part.astype(jnp.float32))
        to_end = jnp.exp(cumul[:, -1:, :] - cumul) * dt_part
        x_weighted = (x_part.astype(jnp.float32) * to_end[..., None]).astype(jnp.bfloat16)
        states = jnp.einsum('cshp,csn->chpn', x_weighted.astype(jnp.float32), b_part.astype(jnp.float32))
        block_decay = jnp.exp(cumul[:, -1, :])

        def advance(carry, item):
            decay, state = item
            return (decay[:, None, None] * carry + state, carry)
        _, before = lax.scan(advance, jnp.zeros((per_group, P_SIZE, N), jnp.float32), (block_decay, states))
        before = before.astype(jnp.bfloat16)
        y_state = jnp.exp(cumul)[..., None] * jnp.einsum('ctn,chpn->cthp', c_part.astype(jnp.float32), before.astype(jnp.float32))
        skip_part = lax.dynamic_slice_in_dim(skip_gain, group * per_group, per_group, 0)
        total = y_intra + y_state + skip_part[None, None, :, None] * x_part.astype(jnp.float32)
        total = total.reshape(TOKENS, width)
        z_part = lax.dynamic_slice_in_dim(z_values, group * width, width, 1).astype(jnp.float32)
        gated = total * jax.nn.silu(z_part)
        scale = lax.rsqrt(lax.optimization_barrier(jnp.mean(gated * gated, axis=1, keepdims=True)) + 1e-05)
        gain_part = lax.dynamic_slice_in_dim(norm_gain, group * width, width, 0)
        return (gated * scale * gain_part[None, :]).astype(jnp.bfloat16)
    normed = lax.map(one_group, jnp.arange(G).astype(jnp.int32))
    normed = jnp.transpose(normed, (1, 0, 2)).reshape(TOKENS, H * P_SIZE)
    return jnp.dot(normed, out_weight, preferred_element_type=jnp.float32).astype(jnp.bfloat16)
```

```python
import functools

import jax
import jax.numpy as jnp
from jax import lax
from jax.experimental import pallas as pl
from jax.experimental.pallas import tpu as pltpu
from jax.sharding import PartitionSpec as P

H = 256
P_SIZE = 64
N = 256
G = 8
KW = 4
BLOCK = 128
MESH = pl.DeviceIdType.MESH


def shifted(value, axis, by):
    devices = lax.axis_size(axis)
    pairs = [(i, i + by) for i in range(devices) if 0 <= i + by < devices]
    return lax.ppermute(value, axis, pairs)


CHUNKS = 4
TILE = 256


def project_kernel(rows, normed_ref, weight_ref, out_ref, w, sent, got, kept, xsent, xgot,
                   wsem, send_sem, recv_sem, xsend_sem, xrecv_sem):
    head = lax.axis_index("head")
    y = head // 2
    x = lax.rem(head, 2)
    wide = out_ref.shape[1] // CHUNKS
    up = {"head": lax.rem(y + 1, 4) * 2 + x}
    down = {"head": lax.rem(y + 3, 4) * 2 + x}
    across = {"head": y * 2 + 1 - x}
    loads = []
    for c in range(CHUNKS):
        load = pltpu.make_async_copy(
            weight_ref.at[:, c * wide : (c + 1) * wide], w.at[c], wsem.at[c]
        )
        load.start()
        loads.append(load)
    barrier = pltpu.get_barrier_semaphore()
    for to in (up, down, across):
        pl.semaphore_signal(barrier, inc=1, device_id=to, device_id_type=MESH)
    pl.semaphore_wait(barrier, 3)

    def ring(c, s, role):
        return pltpu.make_async_remote_copy(
            src_ref=sent.at[c, s, role],
            dst_ref=got.at[c, s, role],
            send_sem=send_sem.at[c, s, role],
            recv_sem=recv_sem.at[c, s, role],
            device_id=up if role == 0 else down,
            device_id_type=MESH,
        )

    def cross(c):
        return pltpu.make_async_remote_copy(
            src_ref=xsent.at[c],
            dst_ref=xgot.at[c],
            send_sem=xsend_sem.at[c],
            recv_sem=xrecv_sem.at[c],
            device_id=across,
            device_id_type=MESH,
        )

    def event(c, s):
        if s == 0:
            if loads[c] is not None:
                loads[c].wait()
        else:
            for role in (0, 1):
                ring(c, s - 1, role).wait_recv()
        block0 = lax.rem(y + 3 - s, 4) * 2 + 1 - x
        block1 = lax.rem(y + 1 + s, 4) * 2 + x
        row0 = pl.multiple_of(block0 * rows, rows)
        row1 = pl.multiple_of(block1 * rows, rows)

        @pl.loop(0, wide // TILE)
        def _(t):
            cols = pl.ds(pl.multiple_of(t * TILE, TILE), TILE)
            left = jnp.concatenate(
                [normed_ref[pl.ds(row0, rows), :], normed_ref[pl.ds(row1, rows), :]], axis=0
            )
            part = jnp.dot(left, w[c, :, cols], preferred_element_type=jnp.float32)
            part0, part1 = part[:rows], part[rows:]
            if s > 0:
                part0 = part0 + got[c, s - 1, 0, :, cols].astype(jnp.float32)
                part1 = part1 + got[c, s - 1, 1, :, cols].astype(jnp.float32)
            if s < 3:
                sent[c, s, 0, :, cols] = part0.astype(jnp.bfloat16)
                sent[c, s, 1, :, cols] = part1.astype(jnp.bfloat16)
            else:
                xsent[c, :, cols] = part0.astype(jnp.bfloat16)
                kept[c, :, cols] = part1

        if s < 3:
            ring(c, s, 0).start()
            ring(c, s, 1).start()
        else:
            cross(c).start()

    def finish(c):
        cross(c).wait_recv()
        out_ref[:, c * wide : (c + 1) * wide] = (
            kept[c] + xgot[c].astype(jnp.float32)
        ).astype(jnp.bfloat16)

    for c, s in ((0, 0), (1, 0), (0, 1), (1, 1), (0, 2), (1, 2), (2, 0), (0, 3), (3, 0), (1, 3),
                 (2, 1), (3, 1), (2, 2), (3, 2), (2, 3), (3, 3)):
        event(c, s)
        if s == 3 and c >= 2:
            finish(c - 2)
    finish(2)
    finish(3)
    for c in range(CHUNKS):
        cross(c).wait_send()
        for s in range(3):
            for role in (0, 1):
                ring(c, s, role).wait_send()


def project(normed, weight):
    tokens, depth = normed.shape
    width = weight.shape[1]
    rows = tokens // 8
    wide = width // CHUNKS
    dma = pltpu.SemaphoreType.DMA
    return pl.pallas_call(
        functools.partial(project_kernel, rows),
        out_shape=jax.ShapeDtypeStruct((rows, width), jnp.bfloat16),
        in_specs=[pl.BlockSpec(memory_space=pltpu.VMEM), pl.BlockSpec(memory_space=pl.ANY)],
        out_specs=pl.BlockSpec(memory_space=pltpu.VMEM),
        scratch_shapes=[
            pltpu.VMEM((CHUNKS, depth, wide), jnp.bfloat16),
            pltpu.VMEM((CHUNKS, 3, 2, rows, wide), jnp.bfloat16),
            pltpu.VMEM((CHUNKS, 3, 2, rows, wide), jnp.bfloat16),
            pltpu.VMEM((CHUNKS, rows, wide), jnp.float32),
            pltpu.VMEM((CHUNKS, rows, wide), jnp.bfloat16),
            pltpu.VMEM((CHUNKS, rows, wide), jnp.bfloat16),
            dma((CHUNKS,)),
            dma((CHUNKS, 3, 2)),
            dma((CHUNKS, 3, 2)),
            dma((CHUNKS,)),
            dma((CHUNKS,)),
        ],
        compiler_params=pltpu.CompilerParams(
            collective_id=1, has_side_effects=True, vmem_limit_bytes=60 * 1024 * 1024
        ),
        name="project",
    )(normed, weight)


def conv_silu(extended, weight, bias, length):
    padded = extended.astype(jnp.float32)
    total = jnp.zeros((length, extended.shape[1]), jnp.float32) + bias[None, :]
    for offset in range(KW):
        total = total + weight[offset][None, :] * padded[offset : offset + length]
    return jax.nn.silu(total).astype(jnp.bfloat16)


def per_device(
    x_values,
    bc_values,
    z_values,
    dt_values,
    xconv_weight,
    bconv_weight,
    xconv_bias,
    bconv_bias,
    dt_offset,
    decay_log,
    skip_gain,
    norm_gain,
    out_weight,
):
    rows_here = x_values.shape[0]
    heads_here = dt_values.shape[1]
    blocks = rows_here // BLOCK
    margin = KW - 1
    prev_x, prev_bc = shifted(
        (x_values[rows_here - margin :], bc_values[:, rows_here - margin :]), "seq", 1
    )
    x_conv = conv_silu(
        jnp.concatenate([prev_x, x_values], axis=0), xconv_weight, xconv_bias, rows_here
    )
    b_conv = conv_silu(
        jnp.concatenate([prev_bc[0], bc_values[0]], axis=0),
        bconv_weight[0],
        bconv_bias[0],
        rows_here,
    )
    c_conv = conv_silu(
        jnp.concatenate([prev_bc[1], bc_values[1]], axis=0),
        bconv_weight[1],
        bconv_bias[1],
        rows_here,
    )
    steps_dt = jax.nn.softplus(dt_values.astype(jnp.float32) + dt_offset[None, :])
    log_decay = steps_dt * (-jnp.exp(decay_log))[None, :]
    x_blocks = x_conv.reshape(blocks, BLOCK, heads_here, P_SIZE)
    b_blocks = b_conv.reshape(blocks, BLOCK, N)
    c_blocks = c_conv.reshape(blocks, BLOCK, N)
    dt_blocks = jnp.transpose(steps_dt.reshape(blocks, BLOCK, heads_here), (0, 2, 1))
    cumul = jnp.cumsum(
        jnp.transpose(log_decay.reshape(blocks, BLOCK, heads_here), (0, 2, 1)), axis=2
    )
    positions = jnp.arange(BLOCK)
    causal = positions[:, None] >= positions[None, :]
    inner = jnp.einsum("ctn,csn->cts", c_blocks, b_blocks, preferred_element_type=jnp.float32)
    diff = cumul[..., :, None] - cumul[..., None, :]
    weights = jnp.where(causal, jnp.exp(jnp.where(causal, diff, 0.0)), 0.0)
    scores = (inner[:, None] * weights * dt_blocks[..., None, :]).astype(jnp.bfloat16)
    y_intra = jnp.einsum("chts,cshp->cthp", scores, x_blocks, preferred_element_type=jnp.float32)
    to_end = jnp.exp(cumul[..., -1:] - cumul) * dt_blocks
    x_weighted = (
        x_blocks.astype(jnp.float32) * jnp.transpose(to_end, (0, 2, 1))[..., None]
    ).astype(jnp.bfloat16)
    states = jnp.einsum("cshp,csn->chpn", x_weighted, b_blocks, preferred_element_type=jnp.float32)
    block_total = cumul[..., -1]
    block_decay = jnp.exp(block_total)
    carry = jnp.zeros((heads_here, P_SIZE, N), jnp.float32)
    local_before = []
    for c in range(blocks):
        local_before.append(carry)
        carry = block_decay[c][..., None, None] * carry + states[c]
    device_decay = jnp.exp(jnp.sum(block_total, axis=0))
    devices = lax.axis_size("seq")
    share = heads_here // devices
    ends = lax.all_to_all(
        carry.astype(jnp.bfloat16).reshape(devices, share, P_SIZE, N), "seq", 0, 0
    )
    decays = lax.all_to_all(device_decay.reshape(devices, share), "seq", 0, 0)
    run = jnp.zeros((share, P_SIZE, N), jnp.float32)
    prefix = []
    for i in range(devices):
        prefix.append(run.astype(jnp.bfloat16))
        run = decays[i][:, None, None] * run + ends[i].astype(jnp.float32)
    incoming = (
        lax.all_to_all(jnp.stack(prefix), "seq", 0, 0)
        .reshape(heads_here, P_SIZE, N)
        .astype(jnp.float32)
    )
    lead = jnp.cumsum(block_total, axis=0) - block_total
    before = (jnp.stack(local_before) + jnp.exp(lead)[..., None, None] * incoming[None]).astype(
        jnp.bfloat16
    )
    y_state = jnp.transpose(jnp.exp(cumul), (0, 2, 1))[..., None] * jnp.einsum(
        "ctn,chpn->cthp", c_blocks, before, preferred_element_type=jnp.float32
    )
    total = y_intra + y_state + skip_gain[None, None, :, None] * x_blocks.astype(jnp.float32)
    width = heads_here * P_SIZE
    gated = total.reshape(rows_here, width) * jax.nn.silu(z_values.astype(jnp.float32))
    scale = lax.rsqrt(jnp.mean(gated * gated, axis=1, keepdims=True) + 1e-05)
    normed = (gated * scale * norm_gain[None, :]).astype(jnp.bfloat16)
    return project(normed, out_weight)


def solution(mesh):
    return jax.shard_map(
        per_device,
        mesh=mesh,
        in_specs=(
            P("seq", "head"),
            P(None, "seq", "head"),
            P("seq", "head"),
            P("seq", "head"),
            P(None, "head"),
            P(None, None, "head"),
            P("head"),
            P(None, "head"),
            P("head"),
            P("head"),
            P("head"),
            P("head"),
            P("head", None),
        ),
        out_specs=P(("seq", "head"), None),
        check_vma=False,
    )
```

```python
import functools

import jax
import jax.numpy as jnp
from jax import lax
from jax.experimental import pallas as pl
from jax.experimental.pallas import tpu as pltpu
from jax.sharding import PartitionSpec as P

H = 256
P_SIZE = 64
N = 256
G = 8
KW = 4
BLOCK = 128
MESH = pl.DeviceIdType.MESH


LOG2E = 1.4426950408889634
FAR = -1e30
F32 = jnp.float32
BF16 = jnp.bfloat16


def dot(left, right, **options):
    return jnp.dot(left, right, preferred_element_type=F32, **options)


def silu(v):
    return 0.5 * v * (1.0 + jnp.tanh(0.5 * v))


def split(v):
    high = v.astype(BF16)
    left = v - high.astype(F32)
    middle = left.astype(BF16)
    low = (left - middle.astype(F32)).astype(BF16)
    return jnp.concatenate([high, middle, low], axis=1)


def spreading(heads):
    shape = (3 * heads, heads * P_SIZE)
    row = lax.broadcasted_iota(jnp.int32, shape, 0)
    lane = lax.broadcasted_iota(jnp.int32, shape, 1)
    hit = lax.rem(row, heads) == lax.shift_right_logical(lane, 6)
    return jnp.where(hit, 1.0, 0.0).astype(BF16)


STEP = 256
SCAN_AFTER = 3


def front_kernel(devices, x_ref, bc_ref, dt_ref, xw_ref, bw_ref, xb_ref, bb_ref, off_ref, dlog_ref,
                 skip_ref, y_hbm, c_ref, lead_ref, incoming_ref,
                 hx, hbc, xf, xc, bt, cumcol, rowt, fend, ec, spread, rowexp, total, carry, before,
                 stage, ends, got, pref, inc,
                 hx_sems, hbc_sems, esend, erecv, psend, precv, ysem):
    me = lax.axis_index("seq")
    tokens, width = x_ref.shape
    blocks = tokens // BLOCK
    heads = dt_ref.shape[1]
    steps = width // STEP
    barrier = pltpu.get_barrier_semaphore()

    @pl.loop(1, devices)
    def _(k):
        pl.semaphore_signal(barrier, inc=1, device_id={"seq": lax.rem(me + k, devices)},
                            device_id_type=MESH)

    pl.semaphore_wait(barrier, devices - 1)

    after = {"seq": lax.rem(me + 1, devices)}
    halo_x = pltpu.make_async_remote_copy(
        src_ref=x_ref.at[tokens - 16 :, :], dst_ref=hx, send_sem=hx_sems.at[0],
        recv_sem=hx_sems.at[1], device_id=after, device_id_type=MESH)
    halo_bc = pltpu.make_async_remote_copy(
        src_ref=bc_ref.at[:, tokens - 16 :, :], dst_ref=hbc, send_sem=hbc_sems.at[0],
        recv_sem=hbc_sems.at[1], device_id=after, device_id_type=MESH)
    halo_bc.start()
    halo_x.start()

    spread[...] = spreading(heads)
    steps_dt = dt_ref[...].astype(F32) + off_ref[...]
    steps_dt = jnp.maximum(steps_dt, 0.0) + jnp.log1p(jnp.exp(-jnp.abs(steps_dt)))
    log_decay = steps_dt * (-LOG2E * jnp.exp(dlog_ref[...]))
    at = lax.broadcasted_iota(jnp.int32, (BLOCK, BLOCK), 0)
    to = lax.broadcasted_iota(jnp.int32, (BLOCK, BLOCK), 1)
    causal = at >= to
    lower = jnp.where(causal, 1.0, 0.0).astype(F32)
    lead = jnp.zeros((1, heads), F32)
    rows_of = []
    for b in range(blocks):
        here = slice(b * BLOCK, (b + 1) * BLOCK)
        dt_here = steps_dt[here]
        cumul = dot(lower, log_decay[here], precision=lax.Precision.HIGHEST)
        end = cumul[BLOCK - 1 :, :]
        cumcol[here, :] = cumul
        rowt[b] = (cumul - LOG2E * jnp.log(dt_here)).T
        fend[here, :] = split(jnp.exp2(end - cumul) * dt_here)
        ec[here, :] = split(jnp.exp2(cumul))
        lead_ref[here, :] = split(jnp.exp2(cumul + lead))
        rows_of.append(jnp.exp2(end))
        lead = lead + end
    rows_of += [jnp.exp2(lead), skip_ref[...]]
    rows_of += [jnp.zeros((1, heads), F32)] * (16 - len(rows_of))
    rowexp[...] = dot(split(jnp.concatenate(rows_of, axis=0)), spread[...])
    whole = rowexp[blocks : blocks + 1, :]
    high = whole.astype(BF16).astype(F32)
    middle = (whole - high).astype(BF16).astype(F32)
    low = whole - high - middle
    row = lax.broadcasted_iota(jnp.int32, (16, width), 0)
    total[...] = jnp.where(
        row == 0, high, jnp.where(row == 1, middle, jnp.where(row == 2, low, 0.0))
    ).astype(BF16)

    first = jnp.where(me > 0, 1.0, 0.0).astype(F32)

    def conv(rows, weights, bias):
        acc = bias + weights[0] * xf[rows + 5 : rows + 5 + BLOCK, :]
        for k in range(1, KW):
            acc = acc + weights[k] * xf[rows + 5 + k : rows + 5 + k + BLOCK, :]
        return silu(acc).astype(BF16)

    halo_bc.wait_recv()
    for i in (0, 1):
        xf[0:8, :] = hbc[i, 8:16, :].astype(F32) * first
        xf[8:, :] = bc_ref[i].astype(F32)
        for b in range(blocks):
            done = conv(b * BLOCK, [bw_ref[i, k : k + 1, :] for k in range(KW)], bb_ref[i : i + 1, :])
            if i == 0:
                bt[b] = done.astype(F32).T.astype(BF16)
            else:
                c_ref[b * BLOCK : (b + 1) * BLOCK, :] = done

    def send_end(owner):
        return pltpu.make_async_remote_copy(
            src_ref=ends.at[owner], dst_ref=got.at[me], send_sem=esend.at[owner],
            recv_sem=erecv.at[me], device_id={"seq": owner}, device_id_type=MESH)

    def send_prefix(target):
        return pltpu.make_async_remote_copy(
            src_ref=pref.at[target], dst_ref=inc.at[me], send_sem=psend.at[target],
            recv_sem=precv.at[me], device_id={"seq": target}, device_id_type=MESH)

    halo_x.wait_recv()

    @pl.loop(0, steps)
    def _(k):
        step = lax.rem(me // 2 + 1 + k, steps)
        lane0 = pl.multiple_of(step * STEP, STEP)
        lanes = pl.ds(lane0, STEP)
        xf[0:8, :] = hx[8:16, lanes].astype(F32) * first
        xf[8:, :] = x_ref[:, lanes].astype(F32)
        weights = [xw_ref[i : i + 1, lanes] for i in range(KW)]
        bias = xb_ref[0:1, lanes]
        carry[...] = jnp.zeros_like(carry)
        for b in range(blocks):
            here = slice(b * BLOCK, (b + 1) * BLOCK)
            done = conv(b * BLOCK, weights, bias)
            xc[here, lanes] = done
            weighted = (done.astype(F32) * dot(fend[here, :], spread[:, lanes])).astype(BF16)
            run = carry[...]
            before[b, :, lanes] = run.astype(BF16)
            carry[...] = rowexp[b : b + 1, lanes] * run + dot(bt[b], weighted)
        for half in (0, 1):
            owner = step * 2 + half
            ends[owner, 0:N, :] = carry[:, half * 128 : (half + 1) * 128].astype(BF16)
            ends[owner, N:, :] = total[:, pl.ds(pl.multiple_of(lane0 + half * 128, 128), 128)]

            @pl.when(owner != me)
            def _():
                send_end(owner).start()

    def store_y(b):
        return pltpu.make_async_copy(
            stage.at[b], y_hbm.at[pl.ds(pl.multiple_of(b * BLOCK, BLOCK), BLOCK), :], ysem.at[b])

    left_half = lax.broadcasted_iota(jnp.int32, (BLOCK, 128), 1) < P_SIZE

    def block_step(b):
        here = pl.ds(pl.multiple_of(b * BLOCK, BLOCK), BLOCK)
        c_here = c_ref[here, :]
        inner = dot(c_here, bt[b])
        for quad in range(steps):
            lanes = slice(quad * STEP, (quad + 1) * STEP)
            sides = []
            for pair in (0, 1):
                scores = []
                for odd in (0, 1):
                    h = quad * 4 + pair * 2 + odd
                    gap = cumcol[here, h : h + 1] - rowt[b, h : h + 1, :]
                    scores.append((inner * jnp.exp2(jnp.where(causal, gap, FAR))).astype(BF16))
                x_here = xc[here, quad * STEP + pair * 128 : quad * STEP + (pair + 1) * 128]
                zero = jnp.zeros_like(x_here)
                both = jnp.concatenate(
                    [jnp.where(left_half, x_here, zero), jnp.where(left_half, zero, x_here)], axis=0)
                sides.append(dot(jnp.concatenate(scores, axis=1), both))
            y = jnp.concatenate(sides, axis=1)
            y = y + dot(ec[here, :], spread[:, lanes]) * dot(c_here, before[b, :, lanes])
            y = y + rowexp[blocks + 1 : blocks + 2, lanes] * xc[here, lanes].astype(F32)
            stage[b, :, lanes] = y
        store_y(b).start()

    pl.loop(0, SCAN_AFTER)(block_step)

    got[me] = ends[me]
    carry[:, :128] = jnp.zeros((N, 128), F32)

    @pl.loop(0, devices)
    def _(i):
        run = carry[:, :128]

        @pl.when(i != me)
        def _():
            pref[i] = run.astype(BF16)
            send_prefix(i).start()
            pltpu.make_async_remote_copy(
                src_ref=ends.at[i], dst_ref=got.at[i], send_sem=esend.at[i], recv_sem=erecv.at[i],
                device_id={"seq": i}, device_id_type=MESH).wait_recv()

        @pl.when(i == me)
        def _():
            inc[me] = run.astype(BF16)

        factor = jnp.sum(got[i, N:, :].astype(F32), axis=0, keepdims=True)
        carry[:, :128] = factor * run + got[i, :N, :].astype(F32)

    pl.loop(SCAN_AFTER, blocks)(block_step)

    @pl.loop(1, devices)
    def _(k):
        other = lax.rem(me + k, devices)
        pltpu.make_async_remote_copy(
            src_ref=pref.at[other], dst_ref=inc.at[other], send_sem=psend.at[other],
            recv_sem=precv.at[other], device_id={"seq": other}, device_id_type=MESH).wait_recv()

    for j in range(devices):
        incoming_ref[:, j * 128 : (j + 1) * 128] = inc[j]

    @pl.loop(1, devices)
    def _(k):
        other = lax.rem(me + k, devices)
        send_end(other).wait_send()
        send_prefix(other).wait_send()

    halo_bc.wait_send()
    halo_x.wait_send()

    @pl.loop(0, blocks)
    def _(b):
        store_y(b).wait()


def front(devices, x, bc, dt, xw, bw, xb, bb, offset, decay_log, skip):
    tokens, width = x.shape
    heads = dt.shape[1]
    blocks = tokens // BLOCK
    dma = pltpu.SemaphoreType.DMA
    vmem = pl.BlockSpec(memory_space=pltpu.VMEM)
    return pl.pallas_call(
        functools.partial(front_kernel, devices),
        out_shape=(
            jax.ShapeDtypeStruct((tokens, width), F32),
            jax.ShapeDtypeStruct((tokens, N), BF16),
            jax.ShapeDtypeStruct((tokens, 3 * heads), BF16),
            jax.ShapeDtypeStruct((N, width), BF16),
        ),
        in_specs=[vmem] * 10,
        out_specs=(pl.BlockSpec(memory_space=pl.ANY), vmem, vmem, vmem),
        scratch_shapes=[
            pltpu.VMEM((16, width), BF16),
            pltpu.VMEM((2, 16, N), BF16),
            pltpu.VMEM((8 + tokens, STEP), F32),
            pltpu.VMEM((tokens, width), BF16),
            pltpu.VMEM((blocks, N, BLOCK), BF16),
            pltpu.VMEM((tokens, heads), F32),
            pltpu.VMEM((blocks, heads, BLOCK), F32),
            pltpu.VMEM((tokens, 3 * heads), BF16),
            pltpu.VMEM((tokens, 3 * heads), BF16),
            pltpu.VMEM((3 * heads, width), BF16),
            pltpu.VMEM((16, width), F32),
            pltpu.VMEM((16, width), BF16),
            pltpu.VMEM((N, STEP), F32),
            pltpu.VMEM((blocks, N, width), BF16),
            pltpu.VMEM((blocks, BLOCK, width), F32),
            pltpu.VMEM((devices, N + 16, 128), BF16),
            pltpu.VMEM((devices, N + 16, 128), BF16),
            pltpu.VMEM((devices, N, 128), BF16),
            pltpu.VMEM((devices, N, 128), BF16),
            dma((2,)),
            dma((2,)),
            dma((devices,)),
            dma((devices,)),
            dma((devices,)),
            dma((devices,)),
            dma((blocks,)),
        ],
        compiler_params=pltpu.CompilerParams(
            collective_id=2, has_side_effects=True, vmem_limit_bytes=60 * 1024 * 1024
        ),
        name="front",
    )(x, bc, dt, xw, bw, xb, bb, offset, decay_log, skip)


CHUNKS = 4
TILE = 256


def project_kernel(rows, y_ref, c_ref, lead_ref, incoming_ref, z_ref, gain_ref, weight_ref, out_ref,
                   ybuf, zbuf, spread, gated, normed, w, sent, got, kept, xsent, xgot,
                   ysem, zsem, wsem, send_sem, recv_sem, xsend_sem, xrecv_sem):
    head = lax.axis_index("head")
    y = head // 2
    x = lax.rem(head, 2)
    wide = out_ref.shape[1] // CHUNKS
    up = {"head": lax.rem(y + 1, 4) * 2 + x}
    down = {"head": lax.rem(y + 3, 4) * 2 + x}
    across = {"head": y * 2 + 1 - x}
    blocks = y_ref.shape[0] // rows
    width = y_ref.shape[1]

    def needed(s):
        return lax.rem(y + 3 - s, 4) * 2 + 1 - x, lax.rem(y + 1 + s, 4) * 2 + x

    def rows_in(s):
        copies = []
        for block in needed(s):
            here = pl.ds(pl.multiple_of(block * rows, rows), rows)
            copies.append(pltpu.make_async_copy(y_ref.at[here, :], ybuf.at[block], ysem.at[block]))
            copies.append(pltpu.make_async_copy(z_ref.at[here, :], zbuf.at[block], zsem.at[block]))
        return copies

    for copy in rows_in(0):
        copy.start()
    loads = []
    for c in range(CHUNKS):
        load = pltpu.make_async_copy(
            weight_ref.at[:, c * wide : (c + 1) * wide], w.at[c], wsem.at[c]
        )
        load.start()
        loads.append(load)
        if c == 0:
            for s in range(1, 4):
                for copy in rows_in(s):
                    copy.start()
    spread[...] = spreading(lead_ref.shape[1] // 3)

    def normalise(block):
        here = pl.ds(pl.multiple_of(block * rows, rows), rows)
        c_here = c_ref[here, :]
        lead_here = lead_ref[here, :]
        square = jnp.zeros((rows, 128), F32)
        for t in range(width // TILE):
            lanes = slice(t * TILE, (t + 1) * TILE)
            y_here = ybuf[block, :, lanes] + dot(lead_here, spread[:, lanes]) * dot(
                c_here, incoming_ref[:, lanes]
            )
            value = y_here * silu(zbuf[block, :, lanes].astype(F32))
            gated[:, lanes] = value
            for part in range(TILE // 128):
                piece = value[:, part * 128 : (part + 1) * 128]
                square = square + piece * piece
        scale = lax.rsqrt(jnp.sum(square, axis=1, keepdims=True) / width + 1e-05)
        for t in range(width // TILE):
            lanes = slice(t * TILE, (t + 1) * TILE)
            normed[here, lanes] = (gated[:, lanes] * scale * gain_ref[:, lanes]).astype(BF16)

    barrier = pltpu.get_barrier_semaphore()
    for to in (up, down, across):
        pl.semaphore_signal(barrier, inc=1, device_id=to, device_id_type=MESH)
    pl.semaphore_wait(barrier, 3)

    def ring(c, s, role):
        return pltpu.make_async_remote_copy(
            src_ref=sent.at[c, s, role],
            dst_ref=got.at[c, s, role],
            send_sem=send_sem.at[c, s, role],
            recv_sem=recv_sem.at[c, s, role],
            device_id=up if role == 0 else down,
            device_id_type=MESH,
        )

    def cross(c):
        return pltpu.make_async_remote_copy(
            src_ref=xsent.at[c],
            dst_ref=xgot.at[c],
            send_sem=xsend_sem.at[c],
            recv_sem=xrecv_sem.at[c],
            device_id=across,
            device_id_type=MESH,
        )

    def event(c, s):
        if s == 0:
            loads[c].wait()
        if c == 0:
            for copy in rows_in(s):
                copy.wait()

            @pl.loop(0, 2)
            def _(role):
                block0, block1 = needed(s)
                normalise(jnp.where(role == 0, block0, block1))

        if s > 0:
            for role in (0, 1):
                ring(c, s - 1, role).wait_recv()
        block0, block1 = needed(s)
        row0 = pl.multiple_of(block0 * rows, rows)
        row1 = pl.multiple_of(block1 * rows, rows)

        @pl.loop(0, wide // TILE)
        def _(t):
            cols = pl.ds(pl.multiple_of(t * TILE, TILE), TILE)
            left = jnp.concatenate(
                [normed[pl.ds(row0, rows), :], normed[pl.ds(row1, rows), :]], axis=0
            )
            part = jnp.dot(left, w[c, :, cols], preferred_element_type=jnp.float32)
            part0, part1 = part[:rows], part[rows:]
            if s > 0:
                part0 = part0 + got[c, s - 1, 0, :, cols].astype(jnp.float32)
                part1 = part1 + got[c, s - 1, 1, :, cols].astype(jnp.float32)
            if s < 3:
                sent[c, s, 0, :, cols] = part0.astype(jnp.bfloat16)
                sent[c, s, 1, :, cols] = part1.astype(jnp.bfloat16)
            else:
                xsent[c, :, cols] = part0.astype(jnp.bfloat16)
                kept[c, :, cols] = part1

        if s < 3:
            ring(c, s, 0).start()
            ring(c, s, 1).start()
        else:
            cross(c).start()

    def finish(c):
        cross(c).wait_recv()
        out_ref[:, c * wide : (c + 1) * wide] = (
            kept[c] + xgot[c].astype(jnp.float32)
        ).astype(jnp.bfloat16)

    for c, s in ((0, 0), (1, 0), (0, 1), (1, 1), (0, 2), (1, 2), (2, 0), (0, 3), (3, 0), (1, 3),
                 (2, 1), (3, 1), (2, 2), (3, 2), (2, 3), (3, 3)):
        event(c, s)
        if s == 3 and c >= 2:
            finish(c - 2)
    finish(2)
    finish(3)
    for c in range(CHUNKS):
        cross(c).wait_send()
        for s in range(3):
            for role in (0, 1):
                ring(c, s, role).wait_send()


def project(y, c_conv, lead, incoming, z, gain, weight):
    tokens, depth = y.shape
    width = weight.shape[1]
    rows = tokens // 8
    wide = width // CHUNKS
    dma = pltpu.SemaphoreType.DMA
    vmem = pl.BlockSpec(memory_space=pltpu.VMEM)
    far = pl.BlockSpec(memory_space=pl.ANY)
    return pl.pallas_call(
        functools.partial(project_kernel, rows),
        out_shape=jax.ShapeDtypeStruct((rows, width), BF16),
        in_specs=[far, vmem, vmem, vmem, far, vmem, far],
        out_specs=vmem,
        scratch_shapes=[
            pltpu.VMEM((8, rows, depth), F32),
            pltpu.VMEM((8, rows, depth), BF16),
            pltpu.VMEM((lead.shape[1], depth), BF16),
            pltpu.VMEM((rows, depth), F32),
            pltpu.VMEM((tokens, depth), BF16),
            pltpu.VMEM((CHUNKS, depth, wide), BF16),
            pltpu.VMEM((CHUNKS, 3, 2, rows, wide), BF16),
            pltpu.VMEM((CHUNKS, 3, 2, rows, wide), BF16),
            pltpu.VMEM((CHUNKS, rows, wide), F32),
            pltpu.VMEM((CHUNKS, rows, wide), BF16),
            pltpu.VMEM((CHUNKS, rows, wide), BF16),
            dma((8,)),
            dma((8,)),
            dma((CHUNKS,)),
            dma((CHUNKS, 3, 2)),
            dma((CHUNKS, 3, 2)),
            dma((CHUNKS,)),
            dma((CHUNKS,)),
        ],
        compiler_params=pltpu.CompilerParams(
            collective_id=1, has_side_effects=True, vmem_limit_bytes=63 * 1024 * 1024
        ),
        name="project",
    )(y, c_conv, lead, incoming, z, gain, weight)


def per_device(
    x_values,
    bc_values,
    z_values,
    dt_values,
    xconv_weight,
    bconv_weight,
    xconv_bias,
    bconv_bias,
    dt_offset,
    decay_log,
    skip_gain,
    norm_gain,
    out_weight,
):
    y, c_conv, lead, incoming = front(
        lax.axis_size("seq"),
        x_values,
        bc_values,
        dt_values,
        xconv_weight,
        bconv_weight,
        xconv_bias[None, :],
        bconv_bias,
        dt_offset[None, :],
        decay_log[None, :],
        skip_gain[None, :],
    )
    return project(y, c_conv, lead, incoming, z_values, norm_gain[None, :], out_weight)


def solution(mesh):
    return jax.shard_map(
        per_device,
        mesh=mesh,
        in_specs=(
            P("seq", "head"),
            P(None, "seq", "head"),
            P("seq", "head"),
            P("seq", "head"),
            P(None, "head"),
            P(None, None, "head"),
            P("head"),
            P(None, "head"),
            P("head"),
            P("head"),
            P("head"),
            P("head"),
            P("head", None),
        ),
        out_specs=P(("seq", "head"), None),
        check_vma=False,
    )
```

```python
import functools

import jax
import jax.numpy as jnp
from jax import lax
from jax.experimental import pallas as pl
from jax.experimental.pallas import tpu as pltpu
from jax.sharding import PartitionSpec as P

H = 256
P_SIZE = 64
N = 256
G = 8
KW = 4
BLOCK = 128
MESH = pl.DeviceIdType.MESH


LOG2E = 1.4426950408889634
FAR = -1e30
F32 = jnp.float32
BF16 = jnp.bfloat16


def dot(left, right, **options):
    return jnp.dot(left, right, preferred_element_type=F32, **options)


def silu(v):
    return 0.5 * v * (1.0 + jnp.tanh(0.5 * v))


def split(v):
    high = v.astype(BF16)
    left = v - high.astype(F32)
    middle = left.astype(BF16)
    low = (left - middle.astype(F32)).astype(BF16)
    return jnp.concatenate([high, middle, low], axis=1)


def spreading(heads):
    shape = (3 * heads, heads * P_SIZE)
    row = lax.broadcasted_iota(jnp.int32, shape, 0)
    lane = lax.broadcasted_iota(jnp.int32, shape, 1)
    hit = lax.rem(row, heads) == lax.shift_right_logical(lane, 6)
    return jnp.where(hit, 1.0, 0.0).astype(BF16)


STEP = 256
SCAN_AFTER = 3


def front_kernel(devices, x_hbm, bc_ref, dtt_ref, xw_ref, bw_ref, xb_ref, bb_ref, off_ref, dlog_ref,
                 skip_ref, y_hbm, c_ref, lead_ref, incoming_ref,
                 x_ref, hx, hbc, xf, xc, bt, cumcol, rowt, fend, ec, spread, rowexp, total, carry, before,
                 stage, ends, got, pref, inc,
                 xin, hx_sems, hbc_sems, esend, erecv, psend, precv, ysem):
    me = lax.axis_index("seq")
    tokens, width = x_ref.shape
    blocks = tokens // BLOCK
    heads = dtt_ref.shape[0]
    steps = width // STEP

    def load_x(step):
        lanes = pl.ds(pl.multiple_of(step * STEP, STEP), STEP)
        return pltpu.make_async_copy(x_hbm.at[:, lanes], x_ref.at[:, lanes], xin.at[step])

    @pl.loop(0, steps)
    def _(k):
        load_x(lax.rem(me // 2 + 1 + k, steps)).start()

    barrier = pltpu.get_barrier_semaphore()

    @pl.loop(1, devices)
    def _(k):
        pl.semaphore_signal(barrier, inc=1, device_id={"seq": lax.rem(me + k, devices)},
                            device_id_type=MESH)

    pl.semaphore_wait(barrier, devices - 1)

    after = {"seq": lax.rem(me + 1, devices)}
    halo_x = pltpu.make_async_remote_copy(
        src_ref=x_hbm.at[tokens - 16 :, :], dst_ref=hx, send_sem=hx_sems.at[0],
        recv_sem=hx_sems.at[1], device_id=after, device_id_type=MESH)
    halo_bc = pltpu.make_async_remote_copy(
        src_ref=bc_ref.at[:, tokens - 16 :, :], dst_ref=hbc, send_sem=hbc_sems.at[0],
        recv_sem=hbc_sems.at[1], device_id=after, device_id_type=MESH)
    halo_bc.start()
    halo_x.start()

    spread[...] = spreading(heads)
    steps_dt = dtt_ref[...].astype(F32).T + off_ref[...]
    steps_dt = jnp.maximum(steps_dt, 0.0) + jnp.log1p(jnp.exp(-jnp.abs(steps_dt)))
    log_decay = steps_dt * (-LOG2E * jnp.exp(dlog_ref[...]))
    at = lax.broadcasted_iota(jnp.int32, (BLOCK, BLOCK), 0)
    to = lax.broadcasted_iota(jnp.int32, (BLOCK, BLOCK), 1)
    causal = at >= to
    lower = jnp.where(causal, 1.0, 0.0).astype(F32)
    lead = jnp.zeros((1, heads), F32)
    rows_of = []
    for b in range(blocks):
        here = slice(b * BLOCK, (b + 1) * BLOCK)
        dt_here = steps_dt[here]
        cumul = dot(lower, log_decay[here], precision=lax.Precision.HIGHEST)
        end = cumul[BLOCK - 1 :, :]
        cumcol[here, :] = cumul
        rowt[b] = (cumul - LOG2E * jnp.log(dt_here)).T
        fend[here, :] = split(jnp.exp2(end - cumul) * dt_here)
        ec[here, :] = split(jnp.exp2(cumul))
        lead_ref[here, :] = split(jnp.exp2(cumul + lead))
        rows_of.append(jnp.exp2(end))
        lead = lead + end
    rows_of += [jnp.exp2(lead), skip_ref[...]]
    rows_of += [jnp.zeros((1, heads), F32)] * (16 - len(rows_of))
    rowexp[...] = dot(split(jnp.concatenate(rows_of, axis=0)), spread[...])
    whole = rowexp[blocks : blocks + 1, :]
    high = whole.astype(BF16).astype(F32)
    middle = (whole - high).astype(BF16).astype(F32)
    low = whole - high - middle
    row = lax.broadcasted_iota(jnp.int32, (16, width), 0)
    total[...] = jnp.where(
        row == 0, high, jnp.where(row == 1, middle, jnp.where(row == 2, low, 0.0))
    ).astype(BF16)

    first = jnp.where(me > 0, 1.0, 0.0).astype(F32)

    def conv(rows, weights, bias):
        acc = bias + weights[0] * xf[rows + 5 : rows + 5 + BLOCK, :]
        for k in range(1, KW):
            acc = acc + weights[k] * xf[rows + 5 + k : rows + 5 + k + BLOCK, :]
        return silu(acc).astype(BF16)

    halo_bc.wait_recv()
    for i in (0, 1):
        xf[0:8, :] = hbc[i, 8:16, :].astype(F32) * first
        xf[8:, :] = bc_ref[i].astype(F32)
        for b in range(blocks):
            done = conv(b * BLOCK, [bw_ref[i, k : k + 1, :] for k in range(KW)], bb_ref[i : i + 1, :])
            if i == 0:
                bt[b] = done.astype(F32).T.astype(BF16)
            else:
                c_ref[b * BLOCK : (b + 1) * BLOCK, :] = done

    def send_end(owner):
        return pltpu.make_async_remote_copy(
            src_ref=ends.at[owner], dst_ref=got.at[me], send_sem=esend.at[owner],
            recv_sem=erecv.at[me], device_id={"seq": owner}, device_id_type=MESH)

    def send_prefix(target):
        return pltpu.make_async_remote_copy(
            src_ref=pref.at[target], dst_ref=inc.at[me], send_sem=psend.at[target],
            recv_sem=precv.at[me], device_id={"seq": target}, device_id_type=MESH)

    halo_x.wait_recv()

    @pl.loop(0, steps)
    def _(k):
        step = lax.rem(me // 2 + 1 + k, steps)
        lane0 = pl.multiple_of(step * STEP, STEP)
        lanes = pl.ds(lane0, STEP)
        load_x(step).wait()
        xf[0:8, :] = hx[8:16, lanes].astype(F32) * first
        xf[8:, :] = x_ref[:, lanes].astype(F32)
        weights = [xw_ref[i : i + 1, lanes] for i in range(KW)]
        bias = xb_ref[0:1, lanes]
        carry[...] = jnp.zeros_like(carry)
        for b in range(blocks):
            here = slice(b * BLOCK, (b + 1) * BLOCK)
            done = conv(b * BLOCK, weights, bias)
            xc[here, lanes] = done
            weighted = (done.astype(F32) * dot(fend[here, :], spread[:, lanes])).astype(BF16)
            run = carry[...]
            before[b, :, lanes] = run.astype(BF16)
            carry[...] = rowexp[b : b + 1, lanes] * run + dot(bt[b], weighted)
        for half in (0, 1):
            owner = step * 2 + half
            ends[owner, 0:N, :] = carry[:, half * 128 : (half + 1) * 128].astype(BF16)
            ends[owner, N:, :] = total[:, pl.ds(pl.multiple_of(lane0 + half * 128, 128), 128)]

            @pl.when(owner != me)
            def _():
                send_end(owner).start()

    def store_y(b):
        return pltpu.make_async_copy(
            stage.at[b], y_hbm.at[pl.ds(pl.multiple_of(b * BLOCK, BLOCK), BLOCK), :], ysem.at[b])

    left_half = lax.broadcasted_iota(jnp.int32, (BLOCK, 128), 1) < P_SIZE

    def block_step(b):
        here = pl.ds(pl.multiple_of(b * BLOCK, BLOCK), BLOCK)
        c_here = c_ref[here, :]
        inner = dot(c_here, bt[b])
        for quad in range(steps):
            lanes = slice(quad * STEP, (quad + 1) * STEP)
            sides = []
            for pair in (0, 1):
                scores = []
                for odd in (0, 1):
                    h = quad * 4 + pair * 2 + odd
                    gap = cumcol[here, h : h + 1] - rowt[b, h : h + 1, :]
                    scores.append((inner * jnp.exp2(jnp.where(causal, gap, FAR))).astype(BF16))
                x_here = xc[here, quad * STEP + pair * 128 : quad * STEP + (pair + 1) * 128]
                zero = jnp.zeros_like(x_here)
                both = jnp.concatenate(
                    [jnp.where(left_half, x_here, zero), jnp.where(left_half, zero, x_here)], axis=0)
                sides.append(dot(jnp.concatenate(scores, axis=1), both))
            y = jnp.concatenate(sides, axis=1)
            y = y + dot(ec[here, :], spread[:, lanes]) * dot(c_here, before[b, :, lanes])
            y = y + rowexp[blocks + 1 : blocks + 2, lanes] * xc[here, lanes].astype(F32)
            stage[b, :, lanes] = y
        store_y(b).start()

    pl.loop(0, SCAN_AFTER)(block_step)

    got[me] = ends[me]
    carry[:, :128] = jnp.zeros((N, 128), F32)

    @pl.loop(0, devices)
    def _(i):
        run = carry[:, :128]

        @pl.when(i != me)
        def _():
            pref[i] = run.astype(BF16)
            send_prefix(i).start()
            pltpu.make_async_remote_copy(
                src_ref=ends.at[i], dst_ref=got.at[i], send_sem=esend.at[i], recv_sem=erecv.at[i],
                device_id={"seq": i}, device_id_type=MESH).wait_recv()

        @pl.when(i == me)
        def _():
            inc[me] = run.astype(BF16)

        factor = jnp.sum(got[i, N:, :].astype(F32), axis=0, keepdims=True)
        carry[:, :128] = factor * run + got[i, :N, :].astype(F32)

    pl.loop(SCAN_AFTER, blocks)(block_step)

    @pl.loop(1, devices)
    def _(k):
        other = lax.rem(me + k, devices)
        pltpu.make_async_remote_copy(
            src_ref=pref.at[other], dst_ref=inc.at[other], send_sem=psend.at[other],
            recv_sem=precv.at[other], device_id={"seq": other}, device_id_type=MESH).wait_recv()

    for j in range(devices):
        incoming_ref[:, j * 128 : (j + 1) * 128] = inc[j]

    @pl.loop(1, devices)
    def _(k):
        other = lax.rem(me + k, devices)
        send_end(other).wait_send()
        send_prefix(other).wait_send()

    halo_bc.wait_send()
    halo_x.wait_send()

    @pl.loop(0, blocks)
    def _(b):
        store_y(b).wait()


def front(devices, x, bc, dt, xw, bw, xb, bb, offset, decay_log, skip):
    tokens, width = x.shape
    heads = dt.shape[0]
    blocks = tokens // BLOCK
    dma = pltpu.SemaphoreType.DMA
    vmem = pl.BlockSpec(memory_space=pltpu.VMEM)
    return pl.pallas_call(
        functools.partial(front_kernel, devices),
        out_shape=(
            jax.ShapeDtypeStruct((tokens, width), F32),
            jax.ShapeDtypeStruct((tokens, N), BF16),
            jax.ShapeDtypeStruct((tokens, 3 * heads), BF16),
            jax.ShapeDtypeStruct((N, width), BF16),
        ),
        in_specs=[pl.BlockSpec(memory_space=pl.ANY)] + [vmem] * 9,
        out_specs=(pl.BlockSpec(memory_space=pl.ANY), vmem, vmem, vmem),
        scratch_shapes=[
            pltpu.VMEM((tokens, width), BF16),
            pltpu.VMEM((16, width), BF16),
            pltpu.VMEM((2, 16, N), BF16),
            pltpu.VMEM((8 + tokens, STEP), F32),
            pltpu.VMEM((tokens, width), BF16),
            pltpu.VMEM((blocks, N, BLOCK), BF16),
            pltpu.VMEM((tokens, heads), F32),
            pltpu.VMEM((blocks, heads, BLOCK), F32),
            pltpu.VMEM((tokens, 3 * heads), BF16),
            pltpu.VMEM((tokens, 3 * heads), BF16),
            pltpu.VMEM((3 * heads, width), BF16),
            pltpu.VMEM((16, width), F32),
            pltpu.VMEM((16, width), BF16),
            pltpu.VMEM((N, STEP), F32),
            pltpu.VMEM((blocks, N, width), BF16),
            pltpu.VMEM((blocks, BLOCK, width), F32),
            pltpu.VMEM((devices, N + 16, 128), BF16),
            pltpu.VMEM((devices, N + 16, 128), BF16),
            pltpu.VMEM((devices, N, 128), BF16),
            pltpu.VMEM((devices, N, 128), BF16),
            dma((width // STEP,)),
            dma((2,)),
            dma((2,)),
            dma((devices,)),
            dma((devices,)),
            dma((devices,)),
            dma((devices,)),
            dma((blocks,)),
        ],
        compiler_params=pltpu.CompilerParams(
            collective_id=2, has_side_effects=True, vmem_limit_bytes=60 * 1024 * 1024
        ),
        name="front",
    )(x, bc, dt, xw, bw, xb, bb, offset, decay_log, skip)


TILE = 256
SIDE = 7 * TILE
HALF = SIDE // 2
CHUNK = 3 * TILE
CHUNKS = 3


def project_kernel(rows, y_ref, c_ref, lead_ref, incoming_ref, z_ref, gain_ref, weight_ref, out_hbm,
                   ybuf, zbuf, spread, gated, normed, wside, w, sent, got, kept, xsent, xgot,
                   sidesent, sidegot, own, turnsent, turngot, out,
                   ysem, zsem, wsem, send_sem, recv_sem, xsend_sem, xrecv_sem,
                   side_send, side_recv, turn_send, turn_recv, osem):
    head = lax.axis_index("head")
    y = head // 2
    x = lax.rem(head, 2)
    up = {"head": lax.rem(y + 1, 4) * 2 + x}
    down = {"head": lax.rem(y + 3, 4) * 2 + x}
    across = {"head": y * 2 + 1 - x}
    width = y_ref.shape[1]

    def needed(s):
        return lax.rem(y + 3 - s, 4) * 2 + 1 - x, lax.rem(y + 1 + s, 4) * 2 + x

    def rows_in(s):
        copies = []
        for block in needed(s):
            here = pl.ds(pl.multiple_of(block * rows, rows), rows)
            copies.append(pltpu.make_async_copy(y_ref.at[here, :], ybuf.at[block], ysem.at[block]))
            copies.append(pltpu.make_async_copy(z_ref.at[here, :], zbuf.at[block], zsem.at[block]))
        return copies

    def column(c):
        return SIDE + c * CHUNK

    def load(c):
        return pltpu.make_async_copy(
            weight_ref.at[:, column(c) : column(c) + CHUNK], w.at[c], wsem.at[c])

    side_load = pltpu.make_async_copy(weight_ref.at[:, :SIDE], wside, wsem.at[CHUNKS])
    for copy in rows_in(0):
        copy.start()
    load(0).start()
    side_load.start()
    for copy in rows_in(1):
        copy.start()
    for c in range(1, CHUNKS):
        load(c).start()
    for s in (2, 3):
        for copy in rows_in(s):
            copy.start()
    spread[...] = spreading(lead_ref.shape[1] // 3)

    def normalise(block):
        here = pl.ds(pl.multiple_of(block * rows, rows), rows)
        c_here = c_ref[here, :]
        lead_here = lead_ref[here, :]
        square = jnp.zeros((rows, 128), F32)
        for t in range(width // TILE):
            lanes = slice(t * TILE, (t + 1) * TILE)
            y_here = ybuf[block, :, lanes] + dot(lead_here, spread[:, lanes]) * dot(
                c_here, incoming_ref[:, lanes]
            )
            value = y_here * silu(zbuf[block, :, lanes].astype(F32))
            gated[:, lanes] = value
            for part in range(TILE // 128):
                piece = value[:, part * 128 : (part + 1) * 128]
                square = square + piece * piece
        scale = lax.rsqrt(jnp.sum(square, axis=1, keepdims=True) / width + 1e-05)
        for t in range(width // TILE):
            lanes = slice(t * TILE, (t + 1) * TILE)
            normed[here, lanes] = (gated[:, lanes] * scale * gain_ref[:, lanes]).astype(BF16)

    def normalise_both(s):
        for copy in rows_in(s):
            copy.wait()
        block0, block1 = needed(s)

        @pl.loop(0, 2)
        def _(role):
            normalise(jnp.where(role == 0, block0, block1))

    barrier = pltpu.get_barrier_semaphore()
    for to in (up, down, across):
        pl.semaphore_signal(barrier, inc=1, device_id=to, device_id_type=MESH)
    pl.semaphore_wait(barrier, 3)

    def ring(c, s, role):
        return pltpu.make_async_remote_copy(
            src_ref=sent.at[c, s, role],
            dst_ref=got.at[c, s, role],
            send_sem=send_sem.at[c, s, role],
            recv_sem=recv_sem.at[c, s, role],
            device_id=up if role == 0 else down,
            device_id_type=MESH,
        )

    def cross(c):
        return pltpu.make_async_remote_copy(
            src_ref=xsent.at[c],
            dst_ref=xgot.at[c],
            send_sem=xsend_sem.at[c],
            recv_sem=xrecv_sem.at[c],
            device_id=across,
            device_id_type=MESH,
        )

    def side_cross(s):
        return pltpu.make_async_remote_copy(
            src_ref=sidesent.at[s],
            dst_ref=sidegot.at[s],
            send_sem=side_send.at[s],
            recv_sem=side_recv.at[s],
            device_id=across,
            device_id_type=MESH,
        )

    def turn(r, way):
        return pltpu.make_async_remote_copy(
            src_ref=turnsent.at[r, way],
            dst_ref=turngot.at[r, way],
            send_sem=turn_send.at[r, way],
            recv_sem=turn_recv.at[r, way],
            device_id=up if way == 0 else down,
            device_id_type=MESH,
        )

    def pair(s, weight):
        row0, row1 = (pl.multiple_of(block * rows, rows) for block in needed(s))
        left = jnp.concatenate(
            [normed[pl.ds(row0, rows), :], normed[pl.ds(row1, rows), :]], axis=0)
        part = dot(left, weight)
        return part[:rows], part[rows:]

    def side_event(s):
        if s == 0:
            side_load.wait()

        @pl.loop(0, SIDE // TILE)
        def _(t):
            cols = pl.ds(pl.multiple_of(t * TILE, TILE), TILE)
            part0, part1 = pair(s, wside[:, cols])
            sidesent[s, :, cols] = part0.astype(BF16)
            own[s, :, cols] = part1

        side_cross(s).start()

    def turn_event(r):
        for s in {0: (0, 2), 1: (1,), 2: (), 3: (3,)}[r]:
            side_cross(s).wait_recv()
        for way in (0, 1):
            cols = slice(way * HALF, (way + 1) * HALF)
            back = (2 - r) % 4
            mine, theirs = (back, r) if way == 0 else (r, back)
            value = own[mine, :, cols] + sidegot[theirs, :, cols].astype(F32)
            if r > 0:
                turn(r - 1, way).wait_recv()
                value = value + turngot[r - 1, way].astype(F32)
            if r < 3:
                turnsent[r, way] = value.astype(BF16)
                turn(r, way).start()
            else:
                out[:, cols] = value.astype(BF16)
        if r == 3:
            store(CHUNKS).start()

    def event(c, s):
        if s == 0:
            load(c).wait()
        else:
            for role in (0, 1):
                ring(c, s - 1, role).wait_recv()

        @pl.loop(0, CHUNK // TILE)
        def _(t):
            cols = pl.ds(pl.multiple_of(t * TILE, TILE), TILE)
            part0, part1 = pair(s, w[c, :, cols])
            if s > 0:
                part0 = part0 + got[c, s - 1, 0, :, cols].astype(F32)
                part1 = part1 + got[c, s - 1, 1, :, cols].astype(F32)
            if s < 3:
                sent[c, s, 0, :, cols] = part0.astype(BF16)
                sent[c, s, 1, :, cols] = part1.astype(BF16)
            else:
                xsent[c, :, cols] = part0.astype(BF16)
                kept[c, :, cols] = part1

        if s < 3:
            ring(c, s, 0).start()
            ring(c, s, 1).start()
        else:
            cross(c).start()

    def store(c):
        cols = slice(0, SIDE) if c == CHUNKS else slice(column(c), column(c) + CHUNK)
        return pltpu.make_async_copy(out.at[:, cols], out_hbm.at[:, cols], osem.at[c])

    def finish(c):
        cross(c).wait_recv()
        out[:, column(c) : column(c) + CHUNK] = (kept[c] + xgot[c].astype(F32)).astype(BF16)
        store(c).start()

    for s in range(3):
        normalise_both(s)
        event(0, s)
        side_event(s)
        event(1, s)
        event(2, s)
    normalise_both(3)
    event(0, 3)
    side_event(3)
    turn_event(0)
    event(1, 3)
    turn_event(1)
    event(2, 3)
    turn_event(2)
    finish(0)
    finish(1)
    turn_event(3)
    finish(2)
    for c in range(CHUNKS):
        cross(c).wait_send()
        for s in range(3):
            for role in (0, 1):
                ring(c, s, role).wait_send()
    for s in range(4):
        side_cross(s).wait_send()
    for r in range(3):
        for way in (0, 1):
            turn(r, way).wait_send()
    for c in range(CHUNKS + 1):
        store(c).wait()


def project(y, c_conv, lead, incoming, z, gain, weight):
    tokens, depth = y.shape
    width = weight.shape[1]
    rows = tokens // 8
    dma = pltpu.SemaphoreType.DMA
    vmem = pl.BlockSpec(memory_space=pltpu.VMEM)
    far = pl.BlockSpec(memory_space=pl.ANY)
    return pl.pallas_call(
        functools.partial(project_kernel, rows),
        out_shape=jax.ShapeDtypeStruct((rows, width), BF16),
        in_specs=[far, vmem, vmem, vmem, far, vmem, far],
        out_specs=far,
        scratch_shapes=[
            pltpu.VMEM((8, rows, depth), F32),
            pltpu.VMEM((8, rows, depth), BF16),
            pltpu.VMEM((lead.shape[1], depth), BF16),
            pltpu.VMEM((rows, depth), F32),
            pltpu.VMEM((tokens, depth), BF16),
            pltpu.VMEM((depth, SIDE), BF16),
            pltpu.VMEM((CHUNKS, depth, CHUNK), BF16),
            pltpu.VMEM((CHUNKS, 3, 2, rows, CHUNK), BF16),
            pltpu.VMEM((CHUNKS, 3, 2, rows, CHUNK), BF16),
            pltpu.VMEM((CHUNKS, rows, CHUNK), F32),
            pltpu.VMEM((CHUNKS, rows, CHUNK), BF16),
            pltpu.VMEM((CHUNKS, rows, CHUNK), BF16),
            pltpu.VMEM((4, rows, SIDE), BF16),
            pltpu.VMEM((4, rows, SIDE), BF16),
            pltpu.VMEM((4, rows, SIDE), F32),
            pltpu.VMEM((3, 2, rows, HALF), BF16),
            pltpu.VMEM((3, 2, rows, HALF), BF16),
            pltpu.VMEM((rows, width), BF16),
            dma((8,)),
            dma((8,)),
            dma((CHUNKS + 1,)),
            dma((CHUNKS, 3, 2)),
            dma((CHUNKS, 3, 2)),
            dma((CHUNKS,)),
            dma((CHUNKS,)),
            dma((4,)),
            dma((4,)),
            dma((3, 2)),
            dma((3, 2)),
            dma((CHUNKS + 1,)),
        ],
        compiler_params=pltpu.CompilerParams(
            collective_id=1, has_side_effects=True, vmem_limit_bytes=63 * 1024 * 1024
        ),
        name="project",
    )(y, c_conv, lead, incoming, z, gain, weight)


def per_device(
    x_values,
    bc_values,
    z_values,
    dt_values,
    xconv_weight,
    bconv_weight,
    xconv_bias,
    bconv_bias,
    dt_offset,
    decay_log,
    skip_gain,
    norm_gain,
    out_weight,
):
    y, c_conv, lead, incoming = front(
        lax.axis_size("seq"),
        x_values,
        bc_values,
        dt_values.T,
        xconv_weight,
        bconv_weight,
        xconv_bias[None, :],
        bconv_bias,
        dt_offset[None, :],
        decay_log[None, :],
        skip_gain[None, :],
    )
    return project(y, c_conv, lead, incoming, z_values, norm_gain[None, :], out_weight)


def solution(mesh):
    return jax.shard_map(
        per_device,
        mesh=mesh,
        in_specs=(
            P("seq", "head"),
            P(None, "seq", "head"),
            P("seq", "head"),
            P("seq", "head"),
            P(None, "head"),
            P(None, None, "head"),
            P("head"),
            P(None, "head"),
            P("head"),
            P("head"),
            P("head"),
            P("head"),
            P("head", None),
        ),
        out_specs=P(("seq", "head"), None),
        check_vma=False,
    )
```

```python
import functools

import jax
import jax.numpy as jnp
from jax import lax
from jax.experimental import pallas as pl
from jax.experimental.pallas import tpu as pltpu
from jax.sharding import PartitionSpec as P

H = 256
P_SIZE = 64
N = 256
G = 8
KW = 4
BLOCK = 128
MESH = pl.DeviceIdType.MESH


LOG2E = 1.4426950408889634
FAR = -1e30
F32 = jnp.float32
BF16 = jnp.bfloat16


def dot(left, right, **options):
    return jnp.dot(left, right, preferred_element_type=F32, **options)


def silu(v):
    return 0.5 * v * (1.0 + jnp.tanh(0.5 * v))


def split(v):
    high = v.astype(BF16)
    left = v - high.astype(F32)
    middle = left.astype(BF16)
    low = (left - middle.astype(F32)).astype(BF16)
    return jnp.concatenate([high, middle, low], axis=1)


def spreading(heads):
    shape = (3 * heads, heads * P_SIZE)
    row = lax.broadcasted_iota(jnp.int32, shape, 0)
    lane = lax.broadcasted_iota(jnp.int32, shape, 1)
    hit = lax.rem(row, heads) == lax.shift_right_logical(lane, 6)
    return jnp.where(hit, 1.0, 0.0).astype(BF16)


STEP = 256
LAG = 3


def front_kernel(devices, x_hbm, bc_ref, dtt_ref, xw_ref, bw_ref, xb_ref, bb_ref, off_ref, dlog_ref,
                 skip_ref, y_hbm, c_ref, lead_ref, incoming_ref,
                 x_ref, hx, hbc, xf, xc, bt, cumcol, rowt, fend, ec, spread, rowexp, leads, factors, carry, before,
                 stage, ends, got, pref, inc,
                 xin, hx_sems, hbc_sems, lead_sems, esend, erecv, psend, precv, ysem):
    me = lax.axis_index("seq")
    tokens, width = x_ref.shape
    blocks = tokens // BLOCK
    heads = dtt_ref.shape[0]
    steps = width // STEP
    share = N // devices

    def load_x(step):
        lanes = pl.ds(pl.multiple_of(step * STEP, STEP), STEP)
        return pltpu.make_async_copy(x_hbm.at[:, lanes], x_ref.at[:, lanes], xin.at[step])

    @pl.loop(0, steps)
    def _(k):
        load_x(k).start()

    barrier = pltpu.get_barrier_semaphore()

    @pl.loop(1, devices)
    def _(k):
        pl.semaphore_signal(barrier, inc=1, device_id={"seq": lax.rem(me + k, devices)},
                            device_id_type=MESH)

    pl.semaphore_wait(barrier, devices - 1)

    after = {"seq": lax.rem(me + 1, devices)}
    halo_x = pltpu.make_async_remote_copy(
        src_ref=x_hbm.at[tokens - 16 :, :], dst_ref=hx, send_sem=hx_sems.at[0],
        recv_sem=hx_sems.at[1], device_id=after, device_id_type=MESH)
    halo_bc = pltpu.make_async_remote_copy(
        src_ref=bc_ref.at[:, tokens - 16 :, :], dst_ref=hbc, send_sem=hbc_sems.at[0],
        recv_sem=hbc_sems.at[1], device_id=after, device_id_type=MESH)
    halo_bc.start()
    halo_x.start()

    spread[...] = spreading(heads)
    steps_dt = dtt_ref[...].astype(F32).T + off_ref[...]
    steps_dt = jnp.maximum(steps_dt, 0.0) + jnp.log1p(jnp.exp(-jnp.abs(steps_dt)))
    log_decay = steps_dt * (-LOG2E * jnp.exp(dlog_ref[...]))
    at = lax.broadcasted_iota(jnp.int32, (BLOCK, BLOCK), 0)
    to = lax.broadcasted_iota(jnp.int32, (BLOCK, BLOCK), 1)
    causal = at >= to
    lower = jnp.where(causal, 1.0, 0.0).astype(F32)
    lead = jnp.zeros((1, heads), F32)
    rows_of = []
    for b in range(blocks):
        here = slice(b * BLOCK, (b + 1) * BLOCK)
        dt_here = steps_dt[here]
        cumul = dot(lower, log_decay[here], precision=lax.Precision.HIGHEST)
        end = cumul[BLOCK - 1 :, :]
        cumcol[here, :] = cumul
        rowt[b] = (cumul - LOG2E * jnp.log(dt_here)).T
        fend[here, :] = split(jnp.exp2(end - cumul) * dt_here)
        ec[here, :] = split(jnp.exp2(cumul))
        lead_ref[here, :] = split(jnp.exp2(cumul + lead))
        rows_of.append(jnp.exp2(end))
        lead = lead + end
    leads[me] = jnp.broadcast_to(
        jnp.concatenate([lead, jnp.zeros((1, 128 - heads), F32)], axis=1), (8, 128))

    def send_lead(target):
        return pltpu.make_async_remote_copy(
            src_ref=leads.at[me], dst_ref=leads.at[me], send_sem=lead_sems.at[0],
            recv_sem=lead_sems.at[1], device_id={"seq": target}, device_id_type=MESH)

    @pl.loop(1, devices)
    def _(k):
        send_lead(lax.rem(me + k, devices)).start()

    rows_of += [skip_ref[...]]
    rows_of += [jnp.zeros((1, heads), F32)] * (16 - len(rows_of))
    rowexp[...] = dot(split(jnp.concatenate(rows_of, axis=0)), spread[...])

    first = jnp.where(me > 0, 1.0, 0.0).astype(F32)

    def conv(rows, weights, bias):
        acc = bias + weights[0] * xf[rows + 5 : rows + 5 + BLOCK, :]
        for k in range(1, KW):
            acc = acc + weights[k] * xf[rows + 5 + k : rows + 5 + k + BLOCK, :]
        return silu(acc).astype(BF16)

    halo_bc.wait_recv()
    for i in (0, 1):
        xf[0:8, :] = hbc[i, 8:16, :].astype(F32) * first
        xf[8:, :] = bc_ref[i].astype(F32)
        for b in range(blocks):
            done = conv(b * BLOCK, [bw_ref[i, k : k + 1, :] for k in range(KW)], bb_ref[i : i + 1, :])
            if i == 0:
                bt[b] = done.astype(F32).T.astype(BF16)
            else:
                c_ref[b * BLOCK : (b + 1) * BLOCK, :] = done

    def part(device):
        return pl.ds(pl.multiple_of(device * share, share), share)

    def send(step, source, target, sends, arrivals, other):
        return pltpu.make_async_remote_copy(
            src_ref=source.at[step, part(other), :], dst_ref=target.at[step, part(me), :],
            send_sem=sends.at[step], recv_sem=arrivals.at[step], device_id={"seq": other},
            device_id_type=MESH)

    def send_all(step, source, target, sends, arrivals):
        @pl.loop(1, devices)
        def _(k):
            send(step, source, target, sends, arrivals, lax.rem(me + k, devices)).start()

        pltpu.make_async_copy(source.at[step, part(me), :], target.at[step, part(me), :],
                              arrivals.at[step]).start()

    def arrived(step, target, sends, arrivals):
        pltpu.make_async_remote_copy(
            src_ref=target.at[step], dst_ref=target.at[step], send_sem=sends.at[step],
            recv_sem=arrivals.at[step], device_id={"seq": me}, device_id_type=MESH).wait_recv()

    def left(step, source, sends, arrivals):
        away = source.at[step, 0 : N - share, :]
        pltpu.make_async_remote_copy(
            src_ref=away, dst_ref=away, send_sem=sends.at[step],
            recv_sem=arrivals.at[step], device_id={"seq": me}, device_id_type=MESH).wait_send()

    def scan(step):
        arrived(step, got, esend, erecv)
        lanes = pl.ds(pl.multiple_of(step * STEP, STEP), STEP)
        run = jnp.zeros((share, STEP), F32)
        for i in range(devices):
            rows = slice(i * share, (i + 1) * share)
            pref[step, rows, :] = run.astype(BF16)
            run = factors[i : i + 1, lanes] * run + got[step, rows, :].astype(F32)
        send_all(step, pref, inc, psend, precv)

    halo_x.wait_recv()

    @pl.loop(0, steps)
    def _(k):
        lanes = pl.ds(pl.multiple_of(k * STEP, STEP), STEP)
        load_x(k).wait()
        xf[0:8, :] = hx[8:16, lanes].astype(F32) * first
        xf[8:, :] = x_ref[:, lanes].astype(F32)
        weights = [xw_ref[i : i + 1, lanes] for i in range(KW)]
        bias = xb_ref[0:1, lanes]
        carry[...] = jnp.zeros_like(carry)
        for b in range(blocks):
            here = slice(b * BLOCK, (b + 1) * BLOCK)
            done = conv(b * BLOCK, weights, bias)
            xc[here, lanes] = done
            weighted = (done.astype(F32) * dot(fend[here, :], spread[:, lanes])).astype(BF16)
            run = carry[...]
            before[b, :, lanes] = run.astype(BF16)
            carry[...] = rowexp[b : b + 1, lanes] * run + dot(bt[b], weighted)
        ends[k] = carry[...].astype(BF16)
        send_all(k, ends, got, esend, erecv)

        @pl.when(k == LAG)
        def _():
            others = leads.at[0 : devices - 1]
            pltpu.make_async_remote_copy(
                src_ref=others, dst_ref=others, send_sem=lead_sems.at[0], recv_sem=lead_sems.at[1],
                device_id={"seq": me}, device_id_type=MESH).wait()
            whole = jnp.concatenate([leads[i, 0:1, :] for i in range(devices)], axis=0)
            factors[...] = dot(split(jnp.exp2(whole[:, :heads])), spread[...])

        @pl.when(k >= LAG)
        def _():
            scan(k - LAG)

    def store_y(b):
        return pltpu.make_async_copy(
            stage.at[b], y_hbm.at[pl.ds(pl.multiple_of(b * BLOCK, BLOCK), BLOCK), :], ysem.at[b])

    left_half = lax.broadcasted_iota(jnp.int32, (BLOCK, 128), 1) < P_SIZE

    def block_step(b):
        here = pl.ds(pl.multiple_of(b * BLOCK, BLOCK), BLOCK)
        c_here = c_ref[here, :]
        inner = dot(c_here, bt[b])
        for quad in range(steps):
            lanes = slice(quad * STEP, (quad + 1) * STEP)
            sides = []
            for pair in (0, 1):
                scores = []
                for odd in (0, 1):
                    h = quad * 4 + pair * 2 + odd
                    gap = cumcol[here, h : h + 1] - rowt[b, h : h + 1, :]
                    scores.append((inner * jnp.exp2(jnp.where(causal, gap, FAR))).astype(BF16))
                x_here = xc[here, quad * STEP + pair * 128 : quad * STEP + (pair + 1) * 128]
                zero = jnp.zeros_like(x_here)
                both = jnp.concatenate(
                    [jnp.where(left_half, x_here, zero), jnp.where(left_half, zero, x_here)], axis=0)
                sides.append(dot(jnp.concatenate(scores, axis=1), both))
            y = jnp.concatenate(sides, axis=1)
            y = y + dot(ec[here, :], spread[:, lanes]) * dot(c_here, before[b, :, lanes])
            y = y + rowexp[blocks : blocks + 1, lanes] * xc[here, lanes].astype(F32)
            stage[b, :, lanes] = y
        store_y(b).start()

    @pl.loop(0, blocks)
    def _(b):
        @pl.when(b < LAG)
        def _():
            scan(steps - LAG + b)

        block_step(b)

    for step in range(steps):
        arrived(step, inc, psend, precv)
        incoming_ref[:, step * STEP : (step + 1) * STEP] = inc[step]
        left(step, ends, esend, erecv)
        left(step, pref, psend, precv)
    halo_bc.wait_send()
    halo_x.wait_send()

    @pl.loop(0, blocks)
    def _(b):
        store_y(b).wait()


def front(devices, x, bc, dt, xw, bw, xb, bb, offset, decay_log, skip):
    tokens, width = x.shape
    heads = dt.shape[0]
    blocks = tokens // BLOCK
    dma = pltpu.SemaphoreType.DMA
    vmem = pl.BlockSpec(memory_space=pltpu.VMEM)
    return pl.pallas_call(
        functools.partial(front_kernel, devices),
        out_shape=(
            jax.ShapeDtypeStruct((tokens, width), F32),
            jax.ShapeDtypeStruct((tokens, N), BF16),
            jax.ShapeDtypeStruct((tokens, 3 * heads), BF16),
            jax.ShapeDtypeStruct((N, width), BF16),
        ),
        in_specs=[pl.BlockSpec(memory_space=pl.ANY)] + [vmem] * 9,
        out_specs=(pl.BlockSpec(memory_space=pl.ANY), vmem, vmem, vmem),
        scratch_shapes=[
            pltpu.VMEM((tokens, width), BF16),
            pltpu.VMEM((16, width), BF16),
            pltpu.VMEM((2, 16, N), BF16),
            pltpu.VMEM((8 + tokens, STEP), F32),
            pltpu.VMEM((tokens, width), BF16),
            pltpu.VMEM((blocks, N, BLOCK), BF16),
            pltpu.VMEM((tokens, heads), F32),
            pltpu.VMEM((blocks, heads, BLOCK), F32),
            pltpu.VMEM((tokens, 3 * heads), BF16),
            pltpu.VMEM((tokens, 3 * heads), BF16),
            pltpu.VMEM((3 * heads, width), BF16),
            pltpu.VMEM((16, width), F32),
            pltpu.VMEM((devices, 8, 128), F32),
            pltpu.VMEM((devices, width), F32),
            pltpu.VMEM((N, STEP), F32),
            pltpu.VMEM((blocks, N, width), BF16),
            pltpu.VMEM((blocks, BLOCK, width), F32),
            pltpu.VMEM((width // STEP, N, STEP), BF16),
            pltpu.VMEM((width // STEP, N, STEP), BF16),
            pltpu.VMEM((width // STEP, N, STEP), BF16),
            pltpu.VMEM((width // STEP, N, STEP), BF16),
            dma((width // STEP,)),
            dma((2,)),
            dma((2,)),
            dma((2,)),
            dma((width // STEP,)),
            dma((width // STEP,)),
            dma((width // STEP,)),
            dma((width // STEP,)),
            dma((blocks,)),
        ],
        compiler_params=pltpu.CompilerParams(
            collective_id=2, has_side_effects=True, vmem_limit_bytes=60 * 1024 * 1024
        ),
        name="front",
    )(x, bc, dt, xw, bw, xb, bb, offset, decay_log, skip)


TILE = 256
SIDE = 7 * TILE
HALF = SIDE // 2
CHUNK = 3 * TILE
CHUNKS = 3


def project_kernel(rows, y_ref, c_ref, lead_ref, incoming_ref, z_ref, gain_ref, weight_ref, out_hbm,
                   ybuf, zbuf, spread, gated, normed, wside, w, sent, got, kept, xsent, xgot,
                   sidesent, sidegot, own, turnsent, turngot, out,
                   ysem, zsem, wsem, send_sem, recv_sem, xsend_sem, xrecv_sem,
                   side_send, side_recv, turn_send, turn_recv, osem):
    head = lax.axis_index("head")
    y = head // 2
    x = lax.rem(head, 2)
    up = {"head": lax.rem(y + 1, 4) * 2 + x}
    down = {"head": lax.rem(y + 3, 4) * 2 + x}
    across = {"head": y * 2 + 1 - x}
    width = y_ref.shape[1]

    def needed(s):
        return lax.rem(y + 3 - s, 4) * 2 + 1 - x, lax.rem(y + 1 + s, 4) * 2 + x

    def rows_in(s):
        copies = []
        for block in needed(s):
            here = pl.ds(pl.multiple_of(block * rows, rows), rows)
            copies.append(pltpu.make_async_copy(y_ref.at[here, :], ybuf.at[block], ysem.at[block]))
            copies.append(pltpu.make_async_copy(z_ref.at[here, :], zbuf.at[block], zsem.at[block]))
        return copies

    def column(c):
        return SIDE + c * CHUNK

    def load(c):
        return pltpu.make_async_copy(
            weight_ref.at[:, column(c) : column(c) + CHUNK], w.at[c], wsem.at[c])

    side_load = pltpu.make_async_copy(weight_ref.at[:, :SIDE], wside, wsem.at[CHUNKS])
    for copy in rows_in(0):
        copy.start()
    load(0).start()
    side_load.start()
    for copy in rows_in(1):
        copy.start()
    for c in range(1, CHUNKS):
        load(c).start()
    for s in (2, 3):
        for copy in rows_in(s):
            copy.start()
    spread[...] = spreading(lead_ref.shape[1] // 3)

    def normalise(block):
        here = pl.ds(pl.multiple_of(block * rows, rows), rows)
        c_here = c_ref[here, :]
        lead_here = lead_ref[here, :]
        square = jnp.zeros((rows, 128), F32)
        for t in range(width // TILE):
            lanes = slice(t * TILE, (t + 1) * TILE)
            y_here = ybuf[block, :, lanes] + dot(lead_here, spread[:, lanes]) * dot(
                c_here, incoming_ref[:, lanes]
            )
            value = y_here * silu(zbuf[block, :, lanes].astype(F32))
            gated[:, lanes] = value
            for part in range(TILE // 128):
                piece = value[:, part * 128 : (part + 1) * 128]
                square = square + piece * piece
        scale = lax.rsqrt(jnp.sum(square, axis=1, keepdims=True) / width + 1e-05)
        for t in range(width // TILE):
            lanes = slice(t * TILE, (t + 1) * TILE)
            normed[here, lanes] = (gated[:, lanes] * scale * gain_ref[:, lanes]).astype(BF16)

    def normalise_both(s):
        for copy in rows_in(s):
            copy.wait()
        block0, block1 = needed(s)

        @pl.loop(0, 2)
        def _(role):
            normalise(jnp.where(role == 0, block0, block1))

    barrier = pltpu.get_barrier_semaphore()
    for to in (up, down, across):
        pl.semaphore_signal(barrier, inc=1, device_id=to, device_id_type=MESH)
    pl.semaphore_wait(barrier, 3)

    def ring(c, s, role):
        return pltpu.make_async_remote_copy(
            src_ref=sent.at[c, s, role],
            dst_ref=got.at[c, s, role],
            send_sem=send_sem.at[c, s, role],
            recv_sem=recv_sem.at[c, s, role],
            device_id=up if role == 0 else down,
            device_id_type=MESH,
        )

    def cross(c):
        return pltpu.make_async_remote_copy(
            src_ref=xsent.at[c],
            dst_ref=xgot.at[c],
            send_sem=xsend_sem.at[c],
            recv_sem=xrecv_sem.at[c],
            device_id=across,
            device_id_type=MESH,
        )

    def side_cross(s):
        return pltpu.make_async_remote_copy(
            src_ref=sidesent.at[s],
            dst_ref=sidegot.at[s],
            send_sem=side_send.at[s],
            recv_sem=side_recv.at[s],
            device_id=across,
            device_id_type=MESH,
        )

    def turn(r, way):
        return pltpu.make_async_remote_copy(
            src_ref=turnsent.at[r, way],
            dst_ref=turngot.at[r, way],
            send_sem=turn_send.at[r, way],
            recv_sem=turn_recv.at[r, way],
            device_id=up if way == 0 else down,
            device_id_type=MESH,
        )

    def pair(s, weight):
        row0, row1 = (pl.multiple_of(block * rows, rows) for block in needed(s))
        left = jnp.concatenate(
            [normed[pl.ds(row0, rows), :], normed[pl.ds(row1, rows), :]], axis=0)
        part = dot(left, weight)
        return part[:rows], part[rows:]

    def side_event(s):
        if s == 0:
            side_load.wait()

        @pl.loop(0, SIDE // TILE)
        def _(t):
            cols = pl.ds(pl.multiple_of(t * TILE, TILE), TILE)
            part0, part1 = pair(s, wside[:, cols])
            sidesent[s, :, cols] = part0.astype(BF16)
            own[s, :, cols] = part1

        side_cross(s).start()

    def turn_event(r):
        for s in {0: (0, 2), 1: (1,), 2: (), 3: (3,)}[r]:
            side_cross(s).wait_recv()
        for way in (0, 1):
            cols = slice(way * HALF, (way + 1) * HALF)
            back = (2 - r) % 4
            mine, theirs = (back, r) if way == 0 else (r, back)
            value = own[mine, :, cols] + sidegot[theirs, :, cols].astype(F32)
            if r > 0:
                turn(r - 1, way).wait_recv()
                value = value + turngot[r - 1, way].astype(F32)
            if r < 3:
                turnsent[r, way] = value.astype(BF16)
                turn(r, way).start()
            else:
                out[:, cols] = value.astype(BF16)
        if r == 3:
            store(CHUNKS).start()

    def event(c, s):
        if s == 0:
            load(c).wait()
        else:
            for role in (0, 1):
                ring(c, s - 1, role).wait_recv()

        @pl.loop(0, CHUNK // TILE)
        def _(t):
            cols = pl.ds(pl.multiple_of(t * TILE, TILE), TILE)
            part0, part1 = pair(s, w[c, :, cols])
            if s > 0:
                part0 = part0 + got[c, s - 1, 0, :, cols].astype(F32)
                part1 = part1 + got[c, s - 1, 1, :, cols].astype(F32)
            if s < 3:
                sent[c, s, 0, :, cols] = part0.astype(BF16)
                sent[c, s, 1, :, cols] = part1.astype(BF16)
            else:
                xsent[c, :, cols] = part0.astype(BF16)
                kept[c, :, cols] = part1

        if s < 3:
            ring(c, s, 0).start()
            ring(c, s, 1).start()
        else:
            cross(c).start()

    def store(c):
        cols = slice(0, SIDE) if c == CHUNKS else slice(column(c), column(c) + CHUNK)
        return pltpu.make_async_copy(out.at[:, cols], out_hbm.at[:, cols], osem.at[c])

    def finish(c):
        cross(c).wait_recv()
        out[:, column(c) : column(c) + CHUNK] = (kept[c] + xgot[c].astype(F32)).astype(BF16)
        store(c).start()

    for s in range(3):
        normalise_both(s)
        event(0, s)
        side_event(s)
        event(1, s)
        event(2, s)
    normalise_both(3)
    event(0, 3)
    side_event(3)
    turn_event(0)
    event(1, 3)
    turn_event(1)
    event(2, 3)
    turn_event(2)
    finish(0)
    finish(1)
    turn_event(3)
    finish(2)
    for c in range(CHUNKS):
        cross(c).wait_send()
        for s in range(3):
            for role in (0, 1):
                ring(c, s, role).wait_send()
    for s in range(4):
        side_cross(s).wait_send()
    for r in range(3):
        for way in (0, 1):
            turn(r, way).wait_send()
    for c in range(CHUNKS + 1):
        store(c).wait()


def project(y, c_conv, lead, incoming, z, gain, weight):
    tokens, depth = y.shape
    width = weight.shape[1]
    rows = tokens // 8
    dma = pltpu.SemaphoreType.DMA
    vmem = pl.BlockSpec(memory_space=pltpu.VMEM)
    far = pl.BlockSpec(memory_space=pl.ANY)
    return pl.pallas_call(
        functools.partial(project_kernel, rows),
        out_shape=jax.ShapeDtypeStruct((rows, width), BF16),
        in_specs=[far, vmem, vmem, vmem, far, vmem, far],
        out_specs=far,
        scratch_shapes=[
            pltpu.VMEM((8, rows, depth), F32),
            pltpu.VMEM((8, rows, depth), BF16),
            pltpu.VMEM((lead.shape[1], depth), BF16),
            pltpu.VMEM((rows, depth), F32),
            pltpu.VMEM((tokens, depth), BF16),
            pltpu.VMEM((depth, SIDE), BF16),
            pltpu.VMEM((CHUNKS, depth, CHUNK), BF16),
            pltpu.VMEM((CHUNKS, 3, 2, rows, CHUNK), BF16),
            pltpu.VMEM((CHUNKS, 3, 2, rows, CHUNK), BF16),
            pltpu.VMEM((CHUNKS, rows, CHUNK), F32),
            pltpu.VMEM((CHUNKS, rows, CHUNK), BF16),
            pltpu.VMEM((CHUNKS, rows, CHUNK), BF16),
            pltpu.VMEM((4, rows, SIDE), BF16),
            pltpu.VMEM((4, rows, SIDE), BF16),
            pltpu.VMEM((4, rows, SIDE), F32),
            pltpu.VMEM((3, 2, rows, HALF), BF16),
            pltpu.VMEM((3, 2, rows, HALF), BF16),
            pltpu.VMEM((rows, width), BF16),
            dma((8,)),
            dma((8,)),
            dma((CHUNKS + 1,)),
            dma((CHUNKS, 3, 2)),
            dma((CHUNKS, 3, 2)),
            dma((CHUNKS,)),
            dma((CHUNKS,)),
            dma((4,)),
            dma((4,)),
            dma((3, 2)),
            dma((3, 2)),
            dma((CHUNKS + 1,)),
        ],
        compiler_params=pltpu.CompilerParams(
            collective_id=1, has_side_effects=True, vmem_limit_bytes=63 * 1024 * 1024
        ),
        name="project",
    )(y, c_conv, lead, incoming, z, gain, weight)


def per_device(
    x_values,
    bc_values,
    z_values,
    dt_values,
    xconv_weight,
    bconv_weight,
    xconv_bias,
    bconv_bias,
    dt_offset,
    decay_log,
    skip_gain,
    norm_gain,
    out_weight,
):
    y, c_conv, lead, incoming = front(
        lax.axis_size("seq"),
        x_values,
        bc_values,
        dt_values.T,
        xconv_weight,
        bconv_weight,
        xconv_bias[None, :],
        bconv_bias,
        dt_offset[None, :],
        decay_log[None, :],
        skip_gain[None, :],
    )
    return project(y, c_conv, lead, incoming, z_values, norm_gain[None, :], out_weight)


def solution(mesh):
    return jax.shard_map(
        per_device,
        mesh=mesh,
        in_specs=(
            P("seq", "head"),
            P(None, "seq", "head"),
            P("seq", "head"),
            P("seq", "head"),
            P(None, "head"),
            P(None, None, "head"),
            P("head"),
            P(None, "head"),
            P("head"),
            P("head"),
            P("head"),
            P("head"),
            P("head", None),
        ),
        out_specs=P(("seq", "head"), None),
        check_vma=False,
    )
```

```python
import functools

import jax
import jax.numpy as jnp
from jax import lax
from jax.experimental import pallas as pl
from jax.experimental.pallas import tpu as pltpu
from jax.sharding import PartitionSpec as P

H = 256
P_SIZE = 64
N = 256
G = 8
KW = 4
BLOCK = 128
MESH = pl.DeviceIdType.MESH


LOG2E = 1.4426950408889634
FAR = -1e30
F32 = jnp.float32
BF16 = jnp.bfloat16


def dot(left, right, **options):
    return jnp.dot(left, right, preferred_element_type=F32, **options)


def silu(v):
    return 0.5 * v * (1.0 + jnp.tanh(0.5 * v))


def split(v):
    high = v.astype(BF16)
    left = v - high.astype(F32)
    middle = left.astype(BF16)
    low = (left - middle.astype(F32)).astype(BF16)
    return jnp.concatenate([high, middle, low], axis=1)


def spreading(heads):
    shape = (3 * heads, heads * P_SIZE)
    row = lax.broadcasted_iota(jnp.int32, shape, 0)
    lane = lax.broadcasted_iota(jnp.int32, shape, 1)
    hit = lax.rem(row, heads) == lax.shift_right_logical(lane, 6)
    return jnp.where(hit, 1.0, 0.0).astype(BF16)


STEP = 256
LAG = 3


def front_kernel(devices, x_hbm, bc_ref, dtt_ref, xw_ref, bw_ref, xb_ref, bb_ref, off_ref, dlog_ref,
                 skip_ref, y_hbm, c_ref, lead_ref, incoming_ref,
                 x_ref, hx, hbc, xf, xc, bt, cumcol, rowt, fend, ec, spread, rowexp, leads, factors, carry, before,
                 stage, ends, got, pref, inc,
                 xin, hx_sems, hbc_sems, lead_sems, esend, erecv, psend, precv, ysem):
    me = lax.axis_index("seq")
    tokens, width = x_ref.shape
    blocks = tokens // BLOCK
    heads = dtt_ref.shape[0]
    steps = width // STEP
    share = N // devices

    def load_x(step):
        lanes = pl.ds(pl.multiple_of(step * STEP, STEP), STEP)
        return pltpu.make_async_copy(x_hbm.at[:, lanes], x_ref.at[:, lanes], xin.at[step])

    @pl.loop(0, steps)
    def _(k):
        load_x(k).start()

    barrier = pltpu.get_barrier_semaphore()

    @pl.loop(1, devices)
    def _(k):
        pl.semaphore_signal(barrier, inc=1, device_id={"seq": lax.rem(me + k, devices)},
                            device_id_type=MESH)

    pl.semaphore_wait(barrier, devices - 1)

    after = {"seq": lax.rem(me + 1, devices)}
    halo_x = pltpu.make_async_remote_copy(
        src_ref=x_hbm.at[tokens - 16 :, :], dst_ref=hx, send_sem=hx_sems.at[0],
        recv_sem=hx_sems.at[1], device_id=after, device_id_type=MESH)
    halo_bc = pltpu.make_async_remote_copy(
        src_ref=bc_ref.at[:, tokens - 16 :, :], dst_ref=hbc, send_sem=hbc_sems.at[0],
        recv_sem=hbc_sems.at[1], device_id=after, device_id_type=MESH)
    halo_bc.start()
    halo_x.start()

    spread[...] = spreading(heads)
    steps_dt = dtt_ref[...].astype(F32) + off_ref[...].T
    steps_dt = jnp.maximum(steps_dt, 0.0) + jnp.log1p(jnp.exp(-jnp.abs(steps_dt)))
    log_dt = LOG2E * jnp.log(steps_dt)
    steps_dt = steps_dt.T
    log_decay = steps_dt * (-LOG2E * jnp.exp(dlog_ref[...]))
    at = lax.broadcasted_iota(jnp.int32, (BLOCK, BLOCK), 0)
    to = lax.broadcasted_iota(jnp.int32, (BLOCK, BLOCK), 1)
    causal = at >= to
    lower = jnp.where(causal, 1.0, 0.0).astype(F32)
    lead = jnp.zeros((1, heads), F32)
    rows_of = []
    for b in range(blocks):
        here = slice(b * BLOCK, (b + 1) * BLOCK)
        dt_here = steps_dt[here]
        cumul = dot(lower, log_decay[here], precision=lax.Precision.HIGHEST)
        end = cumul[BLOCK - 1 :, :]
        cumcol[here, :] = cumul
        rowt[b] = cumul.T - log_dt[:, here]
        fend[here, :] = split(jnp.exp2(end - cumul) * dt_here)
        ec[here, :] = split(jnp.exp2(cumul))
        lead_ref[here, :] = split(jnp.exp2(cumul + lead))
        rows_of.append(jnp.exp2(end))
        lead = lead + end
    leads[me] = jnp.broadcast_to(
        jnp.concatenate([lead, jnp.zeros((1, 128 - heads), F32)], axis=1), (8, 128))

    def send_lead(target):
        return pltpu.make_async_remote_copy(
            src_ref=leads.at[me], dst_ref=leads.at[me], send_sem=lead_sems.at[0],
            recv_sem=lead_sems.at[1], device_id={"seq": target}, device_id_type=MESH)

    @pl.loop(1, devices)
    def _(k):
        send_lead(lax.rem(me + k, devices)).start()

    rows_of += [skip_ref[...]]
    rows_of += [jnp.zeros((1, heads), F32)] * (16 - len(rows_of))
    rowexp[...] = dot(split(jnp.concatenate(rows_of, axis=0)), spread[...])

    first = jnp.where(me > 0, 1.0, 0.0).astype(F32)

    def conv(rows, weights, bias):
        acc = bias + weights[0] * xf[rows + 5 : rows + 5 + BLOCK, :]
        for k in range(1, KW):
            acc = acc + weights[k] * xf[rows + 5 + k : rows + 5 + k + BLOCK, :]
        return silu(acc).astype(BF16)

    halo_bc.wait_recv()
    for i in (0, 1):
        xf[0:8, :] = hbc[i, 8:16, :].astype(F32) * first
        xf[8:, :] = bc_ref[i].astype(F32)
        for b in range(blocks):
            done = conv(b * BLOCK, [bw_ref[i, k : k + 1, :] for k in range(KW)], bb_ref[i : i + 1, :])
            if i == 0:
                bt[b] = done.astype(F32).T.astype(BF16)
            else:
                c_ref[b * BLOCK : (b + 1) * BLOCK, :] = done

    def part(device):
        return pl.ds(pl.multiple_of(device * share, share), share)

    def send(step, source, target, sends, arrivals, other):
        return pltpu.make_async_remote_copy(
            src_ref=source.at[step, part(other), :], dst_ref=target.at[step, part(me), :],
            send_sem=sends.at[step], recv_sem=arrivals.at[step], device_id={"seq": other},
            device_id_type=MESH)

    def send_all(step, source, target, sends, arrivals):
        @pl.loop(1, devices)
        def _(k):
            send(step, source, target, sends, arrivals, lax.rem(me + k, devices)).start()

        pltpu.make_async_copy(source.at[step, part(me), :], target.at[step, part(me), :],
                              arrivals.at[step]).start()

    def arrived(step, target, sends, arrivals):
        pltpu.make_async_remote_copy(
            src_ref=target.at[step], dst_ref=target.at[step], send_sem=sends.at[step],
            recv_sem=arrivals.at[step], device_id={"seq": me}, device_id_type=MESH).wait_recv()

    def left(step, source, sends, arrivals):
        away = source.at[step, 0 : N - share, :]
        pltpu.make_async_remote_copy(
            src_ref=away, dst_ref=away, send_sem=sends.at[step],
            recv_sem=arrivals.at[step], device_id={"seq": me}, device_id_type=MESH).wait_send()

    def scan(step):
        arrived(step, got, esend, erecv)
        lanes = pl.ds(pl.multiple_of(step * STEP, STEP), STEP)
        run = jnp.zeros((share, STEP), F32)
        for i in range(devices):
            rows = slice(i * share, (i + 1) * share)
            pref[step, rows, :] = run.astype(BF16)
            run = factors[i : i + 1, lanes] * run + got[step, rows, :].astype(F32)
        send_all(step, pref, inc, psend, precv)

    halo_x.wait_recv()

    @pl.loop(0, steps)
    def _(k):
        lanes = pl.ds(pl.multiple_of(k * STEP, STEP), STEP)
        load_x(k).wait()
        xf[0:8, :] = hx[8:16, lanes].astype(F32) * first
        xf[8:, :] = x_ref[:, lanes].astype(F32)
        weights = [xw_ref[i : i + 1, lanes] for i in range(KW)]
        bias = xb_ref[0:1, lanes]
        carry[...] = jnp.zeros_like(carry)
        for b in range(blocks):
            here = slice(b * BLOCK, (b + 1) * BLOCK)
            done = conv(b * BLOCK, weights, bias)
            xc[here, lanes] = done
            weighted = (done.astype(F32) * dot(fend[here, :], spread[:, lanes])).astype(BF16)
            run = carry[...]
            before[b, :, lanes] = run.astype(BF16)
            carry[...] = rowexp[b : b + 1, lanes] * run + dot(bt[b], weighted)
        ends[k] = carry[...].astype(BF16)
        send_all(k, ends, got, esend, erecv)

        @pl.when(k == LAG)
        def _():
            others = leads.at[0 : devices - 1]
            pltpu.make_async_remote_copy(
                src_ref=others, dst_ref=others, send_sem=lead_sems.at[0], recv_sem=lead_sems.at[1],
                device_id={"seq": me}, device_id_type=MESH).wait()
            whole = jnp.concatenate([leads[i, 0:1, :] for i in range(devices)], axis=0)
            factors[...] = dot(split(jnp.exp2(whole[:, :heads])), spread[...])

        @pl.when(k >= LAG)
        def _():
            scan(k - LAG)

    def store_y(b):
        return pltpu.make_async_copy(
            stage.at[b], y_hbm.at[pl.ds(pl.multiple_of(b * BLOCK, BLOCK), BLOCK), :], ysem.at[b])

    left_half = lax.broadcasted_iota(jnp.int32, (BLOCK, 128), 1) < P_SIZE

    def block_step(b):
        here = pl.ds(pl.multiple_of(b * BLOCK, BLOCK), BLOCK)
        c_here = c_ref[here, :]
        inner = dot(c_here, bt[b])
        for quad in range(steps):
            lanes = slice(quad * STEP, (quad + 1) * STEP)
            sides = []
            for pair in (0, 1):
                scores = []
                for odd in (0, 1):
                    h = quad * 4 + pair * 2 + odd
                    gap = cumcol[here, h : h + 1] - rowt[b, h : h + 1, :]
                    scores.append((inner * jnp.exp2(jnp.where(causal, gap, FAR))).astype(BF16))
                x_here = xc[here, quad * STEP + pair * 128 : quad * STEP + (pair + 1) * 128]
                zero = jnp.zeros_like(x_here)
                both = jnp.concatenate(
                    [jnp.where(left_half, x_here, zero), jnp.where(left_half, zero, x_here)], axis=0)
                sides.append(dot(jnp.concatenate(scores, axis=1), both))
            y = jnp.concatenate(sides, axis=1)
            y = y + dot(ec[here, :], spread[:, lanes]) * dot(c_here, before[b, :, lanes])
            y = y + rowexp[blocks : blocks + 1, lanes] * xc[here, lanes].astype(F32)
            stage[b, :, lanes] = y
        store_y(b).start()

    @pl.loop(0, blocks)
    def _(b):
        @pl.when(b < LAG)
        def _():
            scan(steps - LAG + b)

        block_step(b)

    for step in range(steps):
        arrived(step, inc, psend, precv)
        incoming_ref[:, step * STEP : (step + 1) * STEP] = inc[step]
        left(step, ends, esend, erecv)
        left(step, pref, psend, precv)
    halo_bc.wait_send()
    halo_x.wait_send()

    @pl.loop(0, blocks)
    def _(b):
        store_y(b).wait()


def front(devices, x, bc, dt, xw, bw, xb, bb, offset, decay_log, skip):
    tokens, width = x.shape
    heads = dt.shape[0]
    blocks = tokens // BLOCK
    dma = pltpu.SemaphoreType.DMA
    vmem = pl.BlockSpec(memory_space=pltpu.VMEM)
    return pl.pallas_call(
        functools.partial(front_kernel, devices),
        out_shape=(
            jax.ShapeDtypeStruct((tokens, width), F32),
            jax.ShapeDtypeStruct((tokens, N), BF16),
            jax.ShapeDtypeStruct((tokens, 3 * heads), BF16),
            jax.ShapeDtypeStruct((N, width), BF16),
        ),
        in_specs=[pl.BlockSpec(memory_space=pl.ANY)] + [vmem] * 9,
        out_specs=(pl.BlockSpec(memory_space=pl.ANY), vmem, vmem, vmem),
        scratch_shapes=[
            pltpu.VMEM((tokens, width), BF16),
            pltpu.VMEM((16, width), BF16),
            pltpu.VMEM((2, 16, N), BF16),
            pltpu.VMEM((8 + tokens, STEP), F32),
            pltpu.VMEM((tokens, width), BF16),
            pltpu.VMEM((blocks, N, BLOCK), BF16),
            pltpu.VMEM((tokens, heads), F32),
            pltpu.VMEM((blocks, heads, BLOCK), F32),
            pltpu.VMEM((tokens, 3 * heads), BF16),
            pltpu.VMEM((tokens, 3 * heads), BF16),
            pltpu.VMEM((3 * heads, width), BF16),
            pltpu.VMEM((16, width), F32),
            pltpu.VMEM((devices, 8, 128), F32),
            pltpu.VMEM((devices, width), F32),
            pltpu.VMEM((N, STEP), F32),
            pltpu.VMEM((blocks, N, width), BF16),
            pltpu.VMEM((blocks, BLOCK, width), F32),
            pltpu.VMEM((width // STEP, N, STEP), BF16),
            pltpu.VMEM((width // STEP, N, STEP), BF16),
            pltpu.VMEM((width // STEP, N, STEP), BF16),
            pltpu.VMEM((width // STEP, N, STEP), BF16),
            dma((width // STEP,)),
            dma((2,)),
            dma((2,)),
            dma((2,)),
            dma((width // STEP,)),
            dma((width // STEP,)),
            dma((width // STEP,)),
            dma((width // STEP,)),
            dma((blocks,)),
        ],
        compiler_params=pltpu.CompilerParams(
            collective_id=2, has_side_effects=True, vmem_limit_bytes=60 * 1024 * 1024
        ),
        name="front",
    )(x, bc, dt, xw, bw, xb, bb, offset, decay_log, skip)


TILE = 256
SIDE = 7 * TILE
HALF = SIDE // 2
CHUNK = 3 * TILE
CHUNKS = 3


def project_kernel(rows, y_ref, c_ref, lead_ref, incoming_ref, z_ref, gain_ref, weight_ref, out_hbm,
                   ybuf, zbuf, spread, gated, normed, wside, w, sent, got, kept, xsent, xgot,
                   sidesent, sidegot, own, turnsent, turngot, out,
                   ysem, zsem, wsem, side_in, send_sem, recv_sem, xsend_sem, xrecv_sem,
                   side_send, side_recv, turn_send, turn_recv, osem):
    head = lax.axis_index("head")
    y = head // 2
    x = lax.rem(head, 2)
    up = {"head": lax.rem(y + 1, 4) * 2 + x}
    down = {"head": lax.rem(y + 3, 4) * 2 + x}
    across = {"head": y * 2 + 1 - x}
    width = y_ref.shape[1]

    def needed(s):
        return lax.rem(y + 3 - s, 4) * 2 + 1 - x, lax.rem(y + 1 + s, 4) * 2 + x

    def rows_in(s):
        copies = []
        for block in needed(s):
            here = pl.ds(pl.multiple_of(block * rows, rows), rows)
            copies.append(pltpu.make_async_copy(y_ref.at[here, :], ybuf.at[block], ysem.at[block]))
            copies.append(pltpu.make_async_copy(z_ref.at[here, :], zbuf.at[block], zsem.at[block]))
        return copies

    def column(c):
        return SIDE + c * CHUNK

    def load(c):
        return pltpu.make_async_copy(
            weight_ref.at[:, column(c) : column(c) + CHUNK], w.at[c], wsem.at[c])

    def side_load(t):
        cols = pl.ds(pl.multiple_of(t * TILE, TILE), TILE)
        return pltpu.make_async_copy(weight_ref.at[:, cols], wside.at[:, cols], side_in.at[t])

    for copy in rows_in(0):
        copy.start()
    load(0).start()
    spread[...] = spreading(lead_ref.shape[1] // 3)

    def normalise(block):
        here = pl.ds(pl.multiple_of(block * rows, rows), rows)
        c_here = c_ref[here, :]
        lead_here = lead_ref[here, :]
        square = jnp.zeros((rows, 128), F32)
        for t in range(width // TILE):
            lanes = slice(t * TILE, (t + 1) * TILE)
            y_here = ybuf[block, :, lanes] + dot(lead_here, spread[:, lanes]) * dot(
                c_here, incoming_ref[:, lanes]
            )
            value = y_here * silu(zbuf[block, :, lanes].astype(F32))
            gated[:, lanes] = value
            for part in range(TILE // 128):
                piece = value[:, part * 128 : (part + 1) * 128]
                square = square + piece * piece
        scale = lax.rsqrt(jnp.sum(square, axis=1, keepdims=True) / width + 1e-05)
        for t in range(width // TILE):
            lanes = slice(t * TILE, (t + 1) * TILE)
            normed[here, lanes] = (gated[:, lanes] * scale * gain_ref[:, lanes]).astype(BF16)

    def normalise_both(s):
        for copy in rows_in(s):
            copy.wait()
        if s == 0:
            for t in range(SIDE // TILE):
                side_load(t).start()
        elif s < 3:
            for copy in rows_in(s + 1):
                copy.start()
        block0, block1 = needed(s)

        @pl.loop(0, 2)
        def _(role):
            normalise(jnp.where(role == 0, block0, block1))

    barrier = pltpu.get_barrier_semaphore()
    for to in (up, down, across):
        pl.semaphore_signal(barrier, inc=1, device_id=to, device_id_type=MESH)
    pl.semaphore_wait(barrier, 3)

    def ring(c, s, role):
        return pltpu.make_async_remote_copy(
            src_ref=sent.at[c, s, role],
            dst_ref=got.at[c, s, role],
            send_sem=send_sem.at[c, s, role],
            recv_sem=recv_sem.at[c, s, role],
            device_id=up if role == 0 else down,
            device_id_type=MESH,
        )

    def cross(c):
        return pltpu.make_async_remote_copy(
            src_ref=xsent.at[c],
            dst_ref=xgot.at[c],
            send_sem=xsend_sem.at[c],
            recv_sem=xrecv_sem.at[c],
            device_id=across,
            device_id_type=MESH,
        )

    def side_cross(s):
        return pltpu.make_async_remote_copy(
            src_ref=sidesent.at[s],
            dst_ref=sidegot.at[s],
            send_sem=side_send.at[s],
            recv_sem=side_recv.at[s],
            device_id=across,
            device_id_type=MESH,
        )

    def turn(r, way):
        return pltpu.make_async_remote_copy(
            src_ref=turnsent.at[r, way],
            dst_ref=turngot.at[r, way],
            send_sem=turn_send.at[r, way],
            recv_sem=turn_recv.at[r, way],
            device_id=up if way == 0 else down,
            device_id_type=MESH,
        )

    def pair(s, weight):
        row0, row1 = (pl.multiple_of(block * rows, rows) for block in needed(s))
        left = jnp.concatenate(
            [normed[pl.ds(row0, rows), :], normed[pl.ds(row1, rows), :]], axis=0)
        part = dot(left, weight)
        return part[:rows], part[rows:]

    def side_event(s):
        @pl.loop(0, SIDE // TILE)
        def _(t):
            if s == 0:
                side_load(t).wait()
            cols = pl.ds(pl.multiple_of(t * TILE, TILE), TILE)
            part0, part1 = pair(s, wside[:, cols])
            sidesent[s, :, cols] = part0.astype(BF16)
            own[s, :, cols] = part1

        side_cross(s).start()

    def turn_event(r):
        for s in {0: (0, 2), 1: (1,), 2: (), 3: (3,)}[r]:
            side_cross(s).wait_recv()
        for way in (0, 1):
            cols = slice(way * HALF, (way + 1) * HALF)
            back = (2 - r) % 4
            mine, theirs = (back, r) if way == 0 else (r, back)
            value = own[mine, :, cols] + sidegot[theirs, :, cols].astype(F32)
            if r > 0:
                turn(r - 1, way).wait_recv()
                value = value + turngot[r - 1, way].astype(F32)
            if r < 3:
                turnsent[r, way] = value.astype(BF16)
                turn(r, way).start()
            else:
                out[:, cols] = value.astype(BF16)
        if r == 3:
            store(CHUNKS).start()

    def event(c, s):
        if s == 0:
            load(c).wait()
            if c == 0:
                load(1).start()
                load(2).start()
            elif c == 1:
                for copy in rows_in(1):
                    copy.start()
        else:
            for role in (0, 1):
                ring(c, s - 1, role).wait_recv()

        @pl.loop(0, CHUNK // TILE)
        def _(t):
            cols = pl.ds(pl.multiple_of(t * TILE, TILE), TILE)
            part0, part1 = pair(s, w[c, :, cols])
            if s > 0:
                part0 = part0 + got[c, s - 1, 0, :, cols].astype(F32)
                part1 = part1 + got[c, s - 1, 1, :, cols].astype(F32)
            if s < 3:
                sent[c, s, 0, :, cols] = part0.astype(BF16)
                sent[c, s, 1, :, cols] = part1.astype(BF16)
            else:
                xsent[c, :, cols] = part0.astype(BF16)
                kept[c, :, cols] = part1

        if s < 3:
            ring(c, s, 0).start()
            ring(c, s, 1).start()
        else:
            cross(c).start()

    def store(c):
        cols = slice(0, SIDE) if c == CHUNKS else slice(column(c), column(c) + CHUNK)
        return pltpu.make_async_copy(out.at[:, cols], out_hbm.at[:, cols], osem.at[c])

    def finish(c):
        cross(c).wait_recv()
        out[:, column(c) : column(c) + CHUNK] = (kept[c] + xgot[c].astype(F32)).astype(BF16)
        store(c).start()

    for s in range(3):
        normalise_both(s)
        event(0, s)
        side_event(s)
        event(1, s)
        event(2, s)
    normalise_both(3)
    event(0, 3)
    side_event(3)
    turn_event(0)
    event(1, 3)
    turn_event(1)
    event(2, 3)
    turn_event(2)
    finish(0)
    finish(1)
    turn_event(3)
    finish(2)
    for c in range(CHUNKS):
        cross(c).wait_send()
        for s in range(3):
            for role in (0, 1):
                ring(c, s, role).wait_send()
    for s in range(4):
        side_cross(s).wait_send()
    for r in range(3):
        for way in (0, 1):
            turn(r, way).wait_send()
    for c in range(CHUNKS + 1):
        store(c).wait()


def project(y, c_conv, lead, incoming, z, gain, weight):
    tokens, depth = y.shape
    width = weight.shape[1]
    rows = tokens // 8
    dma = pltpu.SemaphoreType.DMA
    vmem = pl.BlockSpec(memory_space=pltpu.VMEM)
    far = pl.BlockSpec(memory_space=pl.ANY)
    return pl.pallas_call(
        functools.partial(project_kernel, rows),
        out_shape=jax.ShapeDtypeStruct((rows, width), BF16),
        in_specs=[far, vmem, vmem, vmem, far, vmem, far],
        out_specs=far,
        scratch_shapes=[
            pltpu.VMEM((8, rows, depth), F32),
            pltpu.VMEM((8, rows, depth), BF16),
            pltpu.VMEM((lead.shape[1], depth), BF16),
            pltpu.VMEM((rows, depth), F32),
            pltpu.VMEM((tokens, depth), BF16),
            pltpu.VMEM((depth, SIDE), BF16),
            pltpu.VMEM((CHUNKS, depth, CHUNK), BF16),
            pltpu.VMEM((CHUNKS, 3, 2, rows, CHUNK), BF16),
            pltpu.VMEM((CHUNKS, 3, 2, rows, CHUNK), BF16),
            pltpu.VMEM((CHUNKS, rows, CHUNK), F32),
            pltpu.VMEM((CHUNKS, rows, CHUNK), BF16),
            pltpu.VMEM((CHUNKS, rows, CHUNK), BF16),
            pltpu.VMEM((4, rows, SIDE), BF16),
            pltpu.VMEM((4, rows, SIDE), BF16),
            pltpu.VMEM((4, rows, SIDE), F32),
            pltpu.VMEM((3, 2, rows, HALF), BF16),
            pltpu.VMEM((3, 2, rows, HALF), BF16),
            pltpu.VMEM((rows, width), BF16),
            dma((8,)),
            dma((8,)),
            dma((CHUNKS,)),
            dma((SIDE // TILE,)),
            dma((CHUNKS, 3, 2)),
            dma((CHUNKS, 3, 2)),
            dma((CHUNKS,)),
            dma((CHUNKS,)),
            dma((4,)),
            dma((4,)),
            dma((3, 2)),
            dma((3, 2)),
            dma((CHUNKS + 1,)),
        ],
        compiler_params=pltpu.CompilerParams(
            collective_id=1, has_side_effects=True, vmem_limit_bytes=63 * 1024 * 1024
        ),
        name="project",
    )(y, c_conv, lead, incoming, z, gain, weight)


def per_device(
    x_values,
    bc_values,
    z_values,
    dt_values,
    xconv_weight,
    bconv_weight,
    xconv_bias,
    bconv_bias,
    dt_offset,
    decay_log,
    skip_gain,
    norm_gain,
    out_weight,
):
    y, c_conv, lead, incoming = front(
        lax.axis_size("seq"),
        x_values,
        bc_values,
        dt_values.T,
        xconv_weight,
        bconv_weight,
        xconv_bias[None, :],
        bconv_bias,
        dt_offset[None, :],
        decay_log[None, :],
        skip_gain[None, :],
    )
    return project(y, c_conv, lead, incoming, z_values, norm_gain[None, :], out_weight)


def solution(mesh):
    return jax.shard_map(
        per_device,
        mesh=mesh,
        in_specs=(
            P("seq", "head"),
            P(None, "seq", "head"),
            P("seq", "head"),
            P("seq", "head"),
            P(None, "head"),
            P(None, None, "head"),
            P("head"),
            P(None, "head"),
            P("head"),
            P("head"),
            P("head"),
            P("head"),
            P("head", None),
        ),
        out_specs=P(("seq", "head"), None),
        check_vma=False,
    )
```

```python
import functools

import jax
import jax.numpy as jnp
from jax import lax
from jax.experimental import pallas as pl
from jax.experimental.pallas import tpu as pltpu
from jax.sharding import PartitionSpec as P

H = 256
P_SIZE = 64
N = 256
G = 8
KW = 4
BLOCK = 128
MESH = pl.DeviceIdType.MESH


LOG2E = 1.4426950408889634
FAR = -1e30
F32 = jnp.float32
BF16 = jnp.bfloat16


def dot(left, right, **options):
    return jnp.dot(left, right, preferred_element_type=F32, **options)


def silu(v):
    return 0.5 * v * (1.0 + jnp.tanh(0.5 * v))


def split(v):
    high = v.astype(BF16)
    left = v - high.astype(F32)
    middle = left.astype(BF16)
    low = (left - middle.astype(F32)).astype(BF16)
    return jnp.concatenate([high, middle, low], axis=1)


def spreading(heads):
    shape = (3 * heads, heads * P_SIZE)
    row = lax.broadcasted_iota(jnp.int32, shape, 0)
    lane = lax.broadcasted_iota(jnp.int32, shape, 1)
    hit = lax.rem(row, heads) == lax.shift_right_logical(lane, 6)
    return jnp.where(hit, 1.0, 0.0).astype(BF16)


STEP = 256
LAG = 3


def front_kernel(devices, x_hbm, bc_ref, dtt_ref, xw_ref, bw_ref, xb_ref, bb_ref, off_ref, dlog_ref,
                 skip_ref, y_hbm, c_ref, lead_ref, incoming_ref,
                 x_ref, hx, hbc, xf, xc, bt, cumcol, rowt, fend, ec, spread, rowexp, leads, factors, carry, before,
                 stage, ends, got, pref, inc,
                 xin, hx_sems, hbc_sems, lead_sems, esend, erecv, psend, precv, ysem):
    me = lax.axis_index("seq")
    tokens, width = x_ref.shape
    blocks = tokens // BLOCK
    heads = dtt_ref.shape[0]
    steps = width // STEP
    share = N // devices

    def load_x(step):
        lanes = pl.ds(pl.multiple_of(step * STEP, STEP), STEP)
        return pltpu.make_async_copy(x_hbm.at[:, lanes], x_ref.at[:, lanes], xin.at[step])

    @pl.loop(0, steps)
    def _(k):
        load_x(k).start()

    barrier = pltpu.get_barrier_semaphore()

    @pl.loop(1, devices)
    def _(k):
        pl.semaphore_signal(barrier, inc=1, device_id={"seq": lax.rem(me + k, devices)},
                            device_id_type=MESH)

    pl.semaphore_wait(barrier, devices - 1)

    after = {"seq": lax.rem(me + 1, devices)}
    halo_x = pltpu.make_async_remote_copy(
        src_ref=x_hbm.at[tokens - 16 :, :], dst_ref=hx, send_sem=hx_sems.at[0],
        recv_sem=hx_sems.at[1], device_id=after, device_id_type=MESH)
    halo_bc = pltpu.make_async_remote_copy(
        src_ref=bc_ref.at[:, tokens - 16 :, :], dst_ref=hbc, send_sem=hbc_sems.at[0],
        recv_sem=hbc_sems.at[1], device_id=after, device_id_type=MESH)
    halo_bc.start()
    halo_x.start()

    spread[...] = spreading(heads)
    steps_dt = dtt_ref[...].astype(F32) + off_ref[...].T
    steps_dt = jnp.maximum(steps_dt, 0.0) + jnp.log1p(jnp.exp(-jnp.abs(steps_dt)))
    log_dt = LOG2E * jnp.log(steps_dt)
    steps_dt = steps_dt.T
    log_decay = steps_dt * (-LOG2E * jnp.exp(dlog_ref[...]))
    at = lax.broadcasted_iota(jnp.int32, (BLOCK, BLOCK), 0)
    to = lax.broadcasted_iota(jnp.int32, (BLOCK, BLOCK), 1)
    causal = at >= to
    lower = jnp.where(causal, 1.0, 0.0).astype(F32)
    lead = jnp.zeros((1, heads), F32)
    rows_of = []
    for b in range(blocks):
        here = slice(b * BLOCK, (b + 1) * BLOCK)
        dt_here = steps_dt[here]
        cumul = dot(lower, log_decay[here], precision=lax.Precision.HIGHEST)
        end = cumul[BLOCK - 1 :, :]
        cumcol[here, :] = cumul
        rowt[b] = cumul.T - log_dt[:, here]
        fend[here, :] = split(jnp.exp2(end - cumul) * dt_here)
        ec[here, :] = split(jnp.exp2(cumul))
        lead_ref[here, :] = split(jnp.exp2(cumul + lead))
        rows_of.append(jnp.exp2(end))
        lead = lead + end
    leads[me] = jnp.broadcast_to(
        jnp.concatenate([lead, jnp.zeros((1, 128 - heads), F32)], axis=1), (8, 128))

    def send_lead(target):
        return pltpu.make_async_remote_copy(
            src_ref=leads.at[me], dst_ref=leads.at[me], send_sem=lead_sems.at[0],
            recv_sem=lead_sems.at[1], device_id={"seq": target}, device_id_type=MESH)

    @pl.loop(1, devices)
    def _(k):
        send_lead(lax.rem(me + k, devices)).start()

    rows_of += [skip_ref[...]]
    rows_of += [jnp.zeros((1, heads), F32)] * (16 - len(rows_of))
    rowexp[...] = dot(split(jnp.concatenate(rows_of, axis=0)), spread[...])

    first = jnp.where(me > 0, 1.0, 0.0).astype(F32)

    def conv(rows, weights, bias):
        acc = bias + weights[0] * xf[rows + 5 : rows + 5 + BLOCK, :]
        for k in range(1, KW):
            acc = acc + weights[k] * xf[rows + 5 + k : rows + 5 + k + BLOCK, :]
        return silu(acc).astype(BF16)

    halo_bc.wait_recv()
    for i in (0, 1):
        xf[0:8, :] = hbc[i, 8:16, :].astype(F32) * first
        xf[8:, :] = bc_ref[i].astype(F32)
        for b in range(blocks):
            done = conv(b * BLOCK, [bw_ref[i, k : k + 1, :] for k in range(KW)], bb_ref[i : i + 1, :])
            if i == 0:
                bt[b] = done.astype(F32).T.astype(BF16)
            else:
                c_ref[b * BLOCK : (b + 1) * BLOCK, :] = done

    def part(device):
        return pl.ds(pl.multiple_of(device * share, share), share)

    def send(step, source, target, sends, arrivals, other):
        return pltpu.make_async_remote_copy(
            src_ref=source.at[step, part(other), :], dst_ref=target.at[step, part(me), :],
            send_sem=sends.at[step], recv_sem=arrivals.at[step], device_id={"seq": other},
            device_id_type=MESH)

    def send_all(step, source, target, sends, arrivals):
        @pl.loop(1, devices)
        def _(k):
            send(step, source, target, sends, arrivals, lax.rem(me + k, devices)).start()

        pltpu.make_async_copy(source.at[step, part(me), :], target.at[step, part(me), :],
                              arrivals.at[step]).start()

    def arrived(step, target, sends, arrivals):
        pltpu.make_async_remote_copy(
            src_ref=target.at[step], dst_ref=target.at[step], send_sem=sends.at[step],
            recv_sem=arrivals.at[step], device_id={"seq": me}, device_id_type=MESH).wait_recv()

    def left(step, source, sends, arrivals):
        away = source.at[step, 0 : N - share, :]
        pltpu.make_async_remote_copy(
            src_ref=away, dst_ref=away, send_sem=sends.at[step],
            recv_sem=arrivals.at[step], device_id={"seq": me}, device_id_type=MESH).wait_send()

    def scan(step):
        arrived(step, got, esend, erecv)
        lanes = pl.ds(pl.multiple_of(step * STEP, STEP), STEP)
        run = jnp.zeros((share, STEP), F32)
        for i in range(devices):
            rows = slice(i * share, (i + 1) * share)
            pref[step, rows, :] = run.astype(BF16)
            run = factors[i : i + 1, lanes] * run + got[step, rows, :].astype(F32)
        send_all(step, pref, inc, psend, precv)

    halo_x.wait_recv()

    @pl.loop(0, steps)
    def _(k):
        lanes = pl.ds(pl.multiple_of(k * STEP, STEP), STEP)
        load_x(k).wait()
        xf[0:8, :] = hx[8:16, lanes].astype(F32) * first
        xf[8:, :] = x_ref[:, lanes].astype(F32)
        weights = [xw_ref[i : i + 1, lanes] for i in range(KW)]
        bias = xb_ref[0:1, lanes]
        carry[...] = jnp.zeros_like(carry)
        for b in range(blocks):
            here = slice(b * BLOCK, (b + 1) * BLOCK)
            done = conv(b * BLOCK, weights, bias)
            xc[here, lanes] = done
            weighted = (done.astype(F32) * dot(fend[here, :], spread[:, lanes])).astype(BF16)
            run = carry[...]
            before[b, :, lanes] = run.astype(BF16)
            carry[...] = rowexp[b : b + 1, lanes] * run + dot(bt[b], weighted)
        ends[k] = carry[...].astype(BF16)
        send_all(k, ends, got, esend, erecv)

        @pl.when(k == LAG)
        def _():
            others = leads.at[0 : devices - 1]
            pltpu.make_async_remote_copy(
                src_ref=others, dst_ref=others, send_sem=lead_sems.at[0], recv_sem=lead_sems.at[1],
                device_id={"seq": me}, device_id_type=MESH).wait()
            whole = jnp.concatenate([leads[i, 0:1, :] for i in range(devices)], axis=0)
            factors[...] = dot(split(jnp.exp2(whole[:, :heads])), spread[...])

        @pl.when(k >= LAG)
        def _():
            scan(k - LAG)

    def store_y(b):
        return pltpu.make_async_copy(
            stage.at[b], y_hbm.at[pl.ds(pl.multiple_of(b * BLOCK, BLOCK), BLOCK), :], ysem.at[b])

    left_half = lax.broadcasted_iota(jnp.int32, (BLOCK, 128), 1) < P_SIZE

    def block_step(b):
        here = pl.ds(pl.multiple_of(b * BLOCK, BLOCK), BLOCK)
        c_here = c_ref[here, :]
        inner = dot(c_here, bt[b])
        for quad in range(steps):
            lanes = slice(quad * STEP, (quad + 1) * STEP)
            sides = []
            for pair in (0, 1):
                scores = []
                for odd in (0, 1):
                    h = quad * 4 + pair * 2 + odd
                    gap = cumcol[here, h : h + 1] - rowt[b, h : h + 1, :]
                    scores.append((inner * jnp.exp2(jnp.where(causal, gap, FAR))).astype(BF16))
                x_here = xc[here, quad * STEP + pair * 128 : quad * STEP + (pair + 1) * 128]
                zero = jnp.zeros_like(x_here)
                both = jnp.concatenate(
                    [jnp.where(left_half, x_here, zero), jnp.where(left_half, zero, x_here)], axis=0)
                sides.append(dot(jnp.concatenate(scores, axis=1), both))
            y = jnp.concatenate(sides, axis=1)
            y = y + dot(ec[here, :], spread[:, lanes]) * dot(c_here, before[b, :, lanes])
            y = y + rowexp[blocks : blocks + 1, lanes] * xc[here, lanes].astype(F32)
            stage[b, :, lanes] = y
        store_y(b).start()

    @pl.loop(0, blocks)
    def _(b):
        @pl.when(b < LAG)
        def _():
            scan(steps - LAG + b)

        block_step(b)

    for step in range(steps):
        arrived(step, inc, psend, precv)
        incoming_ref[:, step * STEP : (step + 1) * STEP] = inc[step]
        left(step, ends, esend, erecv)
        left(step, pref, psend, precv)
    halo_bc.wait_send()
    halo_x.wait_send()

    @pl.loop(0, blocks)
    def _(b):
        store_y(b).wait()


def front(devices, x, bc, dt, xw, bw, xb, bb, offset, decay_log, skip):
    tokens, width = x.shape
    heads = dt.shape[0]
    blocks = tokens // BLOCK
    dma = pltpu.SemaphoreType.DMA
    vmem = pl.BlockSpec(memory_space=pltpu.VMEM)
    return pl.pallas_call(
        functools.partial(front_kernel, devices),
        out_shape=(
            jax.ShapeDtypeStruct((tokens, width), F32),
            jax.ShapeDtypeStruct((tokens, N), BF16),
            jax.ShapeDtypeStruct((tokens, 3 * heads), BF16),
            jax.ShapeDtypeStruct((N, width), BF16),
        ),
        in_specs=[pl.BlockSpec(memory_space=pl.ANY)] + [vmem] * 9,
        out_specs=(pl.BlockSpec(memory_space=pl.ANY), vmem, vmem, vmem),
        scratch_shapes=[
            pltpu.VMEM((tokens, width), BF16),
            pltpu.VMEM((16, width), BF16),
            pltpu.VMEM((2, 16, N), BF16),
            pltpu.VMEM((8 + tokens, STEP), F32),
            pltpu.VMEM((tokens, width), BF16),
            pltpu.VMEM((blocks, N, BLOCK), BF16),
            pltpu.VMEM((tokens, heads), F32),
            pltpu.VMEM((blocks, heads, BLOCK), F32),
            pltpu.VMEM((tokens, 3 * heads), BF16),
            pltpu.VMEM((tokens, 3 * heads), BF16),
            pltpu.VMEM((3 * heads, width), BF16),
            pltpu.VMEM((16, width), F32),
            pltpu.VMEM((devices, 8, 128), F32),
            pltpu.VMEM((devices, width), F32),
            pltpu.VMEM((N, STEP), F32),
            pltpu.VMEM((blocks, N, width), BF16),
            pltpu.VMEM((blocks, BLOCK, width), F32),
            pltpu.VMEM((width // STEP, N, STEP), BF16),
            pltpu.VMEM((width // STEP, N, STEP), BF16),
            pltpu.VMEM((width // STEP, N, STEP), BF16),
            pltpu.VMEM((width // STEP, N, STEP), BF16),
            dma((width // STEP,)),
            dma((2,)),
            dma((2,)),
            dma((2,)),
            dma((width // STEP,)),
            dma((width // STEP,)),
            dma((width // STEP,)),
            dma((width // STEP,)),
            dma((blocks,)),
        ],
        compiler_params=pltpu.CompilerParams(
            collective_id=2, has_side_effects=True, vmem_limit_bytes=60 * 1024 * 1024
        ),
        name="front",
    )(x, bc, dt, xw, bw, xb, bb, offset, decay_log, skip)


TILE = 256
SIDE = 7 * TILE
HALF = SIDE // 2
CHUNK = 3 * TILE
CHUNKS = 3


def project_kernel(rows, y_ref, c_ref, lead_ref, incoming_ref, z_ref, gain_ref, weight_ref, out_hbm,
                   ybuf, zbuf, spread, gated, normed, wside, w, sent, got, kept, xsent, xgot,
                   sidesent, sidegot, own, turnsent, turngot, out,
                   ysem, zsem, wsem, side_in, send_sem, recv_sem, xsend_sem, xrecv_sem,
                   side_send, side_recv, turn_send, turn_recv, osem):
    head = lax.axis_index("head")
    y = head // 2
    x = lax.rem(head, 2)
    up = {"head": lax.rem(y + 1, 4) * 2 + x}
    down = {"head": lax.rem(y + 3, 4) * 2 + x}
    across = {"head": y * 2 + 1 - x}
    width = y_ref.shape[1]

    def needed(s):
        return lax.rem(y + 3 - s, 4) * 2 + 1 - x, lax.rem(y + 1 + s, 4) * 2 + x

    def rows_in(s):
        copies = []
        for block in needed(s):
            here = pl.ds(pl.multiple_of(block * rows, rows), rows)
            copies.append(pltpu.make_async_copy(y_ref.at[here, :], ybuf.at[block], ysem.at[block]))
            copies.append(pltpu.make_async_copy(z_ref.at[here, :], zbuf.at[block], zsem.at[block]))
        return copies

    def column(c):
        return SIDE + c * CHUNK

    def load(c):
        return pltpu.make_async_copy(
            weight_ref.at[:, column(c) : column(c) + CHUNK], w.at[c], wsem.at[c])

    def side_load(t):
        cols = pl.ds(pl.multiple_of(t * TILE, TILE), TILE)
        return pltpu.make_async_copy(weight_ref.at[:, cols], wside.at[:, cols], side_in.at[t])

    for copy in rows_in(0):
        copy.start()
    load(0).start()
    spread[...] = spreading(lead_ref.shape[1] // 3)

    def normalise(block):
        here = pl.ds(pl.multiple_of(block * rows, rows), rows)
        c_here = c_ref[here, :]
        lead_here = lead_ref[here, :]
        square = jnp.zeros((rows, 128), F32)
        for t in range(width // TILE):
            lanes = slice(t * TILE, (t + 1) * TILE)
            y_here = ybuf[block, :, lanes] + dot(lead_here, spread[:, lanes]) * dot(
                c_here, incoming_ref[:, lanes]
            )
            value = y_here * silu(zbuf[block, :, lanes].astype(F32))
            gated[:, lanes] = value
            for part in range(TILE // 128):
                piece = value[:, part * 128 : (part + 1) * 128]
                square = square + piece * piece
        scale = lax.rsqrt(jnp.sum(square, axis=1, keepdims=True) / width + 1e-05)
        for t in range(width // TILE):
            lanes = slice(t * TILE, (t + 1) * TILE)
            normed[here, lanes] = (gated[:, lanes] * scale * gain_ref[:, lanes]).astype(BF16)

    def normalise_both(s):
        for copy in rows_in(s):
            copy.wait()
        if s == 0:
            for t in range(SIDE // TILE):
                side_load(t).start()
        elif s < 3:
            for copy in rows_in(s + 1):
                copy.start()
        block0, block1 = needed(s)

        @pl.loop(0, 2)
        def _(role):
            normalise(jnp.where(role == 0, block0, block1))

    barrier = pltpu.get_barrier_semaphore()
    for to in (up, down, across):
        pl.semaphore_signal(barrier, inc=1, device_id=to, device_id_type=MESH)
    pl.semaphore_wait(barrier, 3)

    def ring(c, s, role):
        return pltpu.make_async_remote_copy(
            src_ref=sent.at[c, s, role],
            dst_ref=got.at[c, s, role],
            send_sem=send_sem.at[c, s, role],
            recv_sem=recv_sem.at[c, s, role],
            device_id=up if role == 0 else down,
            device_id_type=MESH,
        )

    def cross(c):
        return pltpu.make_async_remote_copy(
            src_ref=xsent.at[c],
            dst_ref=xgot.at[c],
            send_sem=xsend_sem.at[c],
            recv_sem=xrecv_sem.at[c],
            device_id=across,
            device_id_type=MESH,
        )

    def side_cross(s):
        return pltpu.make_async_remote_copy(
            src_ref=sidesent.at[s],
            dst_ref=sidegot.at[s],
            send_sem=side_send.at[s],
            recv_sem=side_recv.at[s],
            device_id=across,
            device_id_type=MESH,
        )

    def turn(r, way):
        return pltpu.make_async_remote_copy(
            src_ref=turnsent.at[r, way],
            dst_ref=turngot.at[r, way],
            send_sem=turn_send.at[r, way],
            recv_sem=turn_recv.at[r, way],
            device_id=up if way == 0 else down,
            device_id_type=MESH,
        )

    def pair(s, weight):
        row0, row1 = (pl.multiple_of(block * rows, rows) for block in needed(s))
        left = jnp.concatenate(
            [normed[pl.ds(row0, rows), :], normed[pl.ds(row1, rows), :]], axis=0)
        part = dot(left, weight)
        return part[:rows], part[rows:]

    def side_event(s):
        @pl.loop(0, SIDE // TILE)
        def _(t):
            if s == 0:
                side_load(t).wait()
            cols = pl.ds(pl.multiple_of(t * TILE, TILE), TILE)
            part0, part1 = pair(s, wside[:, cols])
            sidesent[s, :, cols] = part0.astype(BF16)
            own[s, :, cols] = part1

        side_cross(s).start()

    def turn_event(r):
        for s in {0: (0, 2), 1: (1,), 2: (), 3: (3,)}[r]:
            side_cross(s).wait_recv()
        for way in (0, 1):
            cols = slice(way * HALF, (way + 1) * HALF)
            back = (2 - r) % 4
            mine, theirs = (back, r) if way == 0 else (r, back)
            value = own[mine, :, cols] + sidegot[theirs, :, cols].astype(F32)
            if r > 0:
                turn(r - 1, way).wait_recv()
                value = value + turngot[r - 1, way].astype(F32)
            if r < 3:
                turnsent[r, way] = value.astype(BF16)
                turn(r, way).start()
            else:
                out[:, cols] = value.astype(BF16)
        if r == 3:
            store(CHUNKS).start()

    def event(c, s):
        if s == 0:
            load(c).wait()
            if c == 0:
                load(1).start()
                load(2).start()
            elif c == 1:
                for copy in rows_in(1):
                    copy.start()
        else:
            for role in (0, 1):
                ring(c, s - 1, role).wait_recv()

        @pl.loop(0, CHUNK // TILE)
        def _(t):
            cols = pl.ds(pl.multiple_of(t * TILE, TILE), TILE)
            part0, part1 = pair(s, w[c, :, cols])
            if s > 0:
                part0 = part0 + got[c, s - 1, 0, :, cols].astype(F32)
                part1 = part1 + got[c, s - 1, 1, :, cols].astype(F32)
            if s < 3:
                sent[c, s, 0, :, cols] = part0.astype(BF16)
                sent[c, s, 1, :, cols] = part1.astype(BF16)
            else:
                xsent[c, :, cols] = part0.astype(BF16)
                kept[c, :, cols] = part1

        if s < 3:
            ring(c, s, 0).start()
            ring(c, s, 1).start()
        else:
            cross(c).start()

    def store(c):
        cols = slice(0, SIDE) if c == CHUNKS else slice(column(c), column(c) + CHUNK)
        return pltpu.make_async_copy(out.at[:, cols], out_hbm.at[:, cols], osem.at[c])

    def finish(c):
        cross(c).wait_recv()
        out[:, column(c) : column(c) + CHUNK] = (kept[c] + xgot[c].astype(F32)).astype(BF16)
        store(c).start()

    for s in range(3):
        normalise_both(s)
        event(0, s)
        side_event(s)
        event(1, s)
        event(2, s)
    normalise_both(3)
    event(0, 3)
    turn_event(0)
    side_event(3)
    turn_event(1)
    event(1, 3)
    turn_event(2)
    event(2, 3)
    finish(0)
    finish(1)
    turn_event(3)
    finish(2)
    for c in range(CHUNKS):
        cross(c).wait_send()
        for s in range(3):
            for role in (0, 1):
                ring(c, s, role).wait_send()
    for s in range(4):
        side_cross(s).wait_send()
    for r in range(3):
        for way in (0, 1):
            turn(r, way).wait_send()
    for c in range(CHUNKS + 1):
        store(c).wait()


def project(y, c_conv, lead, incoming, z, gain, weight):
    tokens, depth = y.shape
    width = weight.shape[1]
    rows = tokens // 8
    dma = pltpu.SemaphoreType.DMA
    vmem = pl.BlockSpec(memory_space=pltpu.VMEM)
    far = pl.BlockSpec(memory_space=pl.ANY)
    return pl.pallas_call(
        functools.partial(project_kernel, rows),
        out_shape=jax.ShapeDtypeStruct((rows, width), BF16),
        in_specs=[far, vmem, vmem, vmem, far, vmem, far],
        out_specs=far,
        scratch_shapes=[
            pltpu.VMEM((8, rows, depth), F32),
            pltpu.VMEM((8, rows, depth), BF16),
            pltpu.VMEM((lead.shape[1], depth), BF16),
            pltpu.VMEM((rows, depth), F32),
            pltpu.VMEM((tokens, depth), BF16),
            pltpu.VMEM((depth, SIDE), BF16),
            pltpu.VMEM((CHUNKS, depth, CHUNK), BF16),
            pltpu.VMEM((CHUNKS, 3, 2, rows, CHUNK), BF16),
            pltpu.VMEM((CHUNKS, 3, 2, rows, CHUNK), BF16),
            pltpu.VMEM((CHUNKS, rows, CHUNK), F32),
            pltpu.VMEM((CHUNKS, rows, CHUNK), BF16),
            pltpu.VMEM((CHUNKS, rows, CHUNK), BF16),
            pltpu.VMEM((4, rows, SIDE), BF16),
            pltpu.VMEM((4, rows, SIDE), BF16),
            pltpu.VMEM((4, rows, SIDE), F32),
            pltpu.VMEM((3, 2, rows, HALF), BF16),
            pltpu.VMEM((3, 2, rows, HALF), BF16),
            pltpu.VMEM((rows, width), BF16),
            dma((8,)),
            dma((8,)),
            dma((CHUNKS,)),
            dma((SIDE // TILE,)),
            dma((CHUNKS, 3, 2)),
            dma((CHUNKS, 3, 2)),
            dma((CHUNKS,)),
            dma((CHUNKS,)),
            dma((4,)),
            dma((4,)),
            dma((3, 2)),
            dma((3, 2)),
            dma((CHUNKS + 1,)),
        ],
        compiler_params=pltpu.CompilerParams(
            collective_id=1, has_side_effects=True, vmem_limit_bytes=63 * 1024 * 1024
        ),
        name="project",
    )(y, c_conv, lead, incoming, z, gain, weight)


def per_device(
    x_values,
    bc_values,
    z_values,
    dt_values,
    xconv_weight,
    bconv_weight,
    xconv_bias,
    bconv_bias,
    dt_offset,
    decay_log,
    skip_gain,
    norm_gain,
    out_weight,
):
    y, c_conv, lead, incoming = front(
        lax.axis_size("seq"),
        x_values,
        bc_values,
        dt_values.T,
        xconv_weight,
        bconv_weight,
        xconv_bias[None, :],
        bconv_bias,
        dt_offset[None, :],
        decay_log[None, :],
        skip_gain[None, :],
    )
    return project(y, c_conv, lead, incoming, z_values, norm_gain[None, :], out_weight)


def solution(mesh):
    return jax.shard_map(
        per_device,
        mesh=mesh,
        in_specs=(
            P("seq", "head"),
            P(None, "seq", "head"),
            P("seq", "head"),
            P("seq", "head"),
            P(None, "head"),
            P(None, None, "head"),
            P("head"),
            P(None, "head"),
            P("head"),
            P("head"),
            P("head"),
            P("head"),
            P("head", None),
        ),
        out_specs=P(("seq", "head"), None),
        check_vma=False,
    )
```
